512 devices in a mesh: rows: 64 (over z, y), cls: 8 (over x, core).
Axes of the slice: x: 4, y: 4, z: 16, core: 2. Of those that a mesh axis runs over, the one named last changes fastest.
Arguments:
- logits: float32 [262144, 1024], P('rows', 'cls'), may hold values from -24 to 360, as said below
- leaf_index: int32 [262144], P('rows'), may hold values from 0 to 127
- labels: int32 [262144], P('rows'), may hold values from 0 to 1023
Outputs:
- leaf_values: float32 [128, 1024], P(None, 'cls')
- updated: float32 [262144, 1024], P('rows', 'cls')
The draws below stay inside these ranges and needn't reach their ends.
Inputs may be any that keep to these rules, and one draw needn't show every extreme that they name: `logits`: raw scores of a model in training.
All inputs are finite; a program needn't handle non-finite values.
Results may differ from the reference program's by a relative error of at most 0.0003.
Values sent between devices are 32-bit elements; how exact they have to be, the bound alone decides.
A program may use at most 64 MiB of HBM per device.

```python
import jax
import jax.numpy as jnp
from jax import lax

C = 1024
LEAVES = 128
ROW_DEV = 4096
ROWS = 262144
N_ROWS = 64


def draw_logits(key, part):
    first = jax.random.fold_in(key, 0)
    return jnp.clip(3.0 * jax.random.normal(first, (ROWS, C), jnp.float32), -24.0, 24.0)


def touch_ends(array, own_key, least, largest):
    extent = array.shape
    index_at = [jax.random.randint(jax.random.fold_in(own_key, axis), (), 0, extent[axis]) for axis in range(len(extent))]
    array = array.at[tuple(index_at)].set(least)
    longest = extent.index(max(extent))
    index_at[longest] = (index_at[longest] + 1) % extent[longest]
    return array.at[tuple(index_at)].set(largest)


def setup_inputs(seed: int = 0) -> dict:
    keys = jax.random.split(jax.random.key(seed), 4)
    logits = draw_logits(jax.random.fold_in(keys[3], 71), 0)
    leaf_index = touch_ends(jax.random.randint(keys[1], (ROWS,), 0, LEAVES), jax.random.fold_in(keys[1], 1), 0, LEAVES - 1).astype(jnp.int32)
    labels = touch_ends(jax.random.randint(keys[2], (ROWS,), 0, C), jax.random.fold_in(keys[2], 1), 0, C - 1).astype(jnp.int32)
    return dict(logits=logits, leaf_index=leaf_index, labels=labels)


def block_terms(block_logits, block_leaf, block_label):
    peak = jnp.max(block_logits, axis=1, keepdims=True)
    expo = jnp.exp(block_logits - peak)
    total = jnp.sum(expo, axis=1, keepdims=True)
    prob = expo / total
    classes = jnp.arange(C, dtype=jnp.int32)[None, :]
    grad = prob - (block_label[:, None] == classes).astype(jnp.float32)
    hess = prob * (1.0 - prob)
    leaves = jnp.arange(LEAVES, dtype=jnp.int32)[None, :]
    onehot = (block_leaf[:, None] == leaves).astype(jnp.float32)
    dims = (((0,), (0,)), ((), ()))
    g_sum = lax.dot_general(onehot, grad, dims, precision=lax.Precision.HIGHEST, preferred_element_type=jnp.float32)
    h_sum = lax.dot_general(onehot, hess, dims, precision=lax.Precision.HIGHEST, preferred_element_type=jnp.float32)
    return g_sum, h_sum


def reference(logits, leaf_index, labels):
    blocks = logits.reshape(N_ROWS, ROW_DEV, C)
    leaf_blocks = leaf_index.reshape(N_ROWS, ROW_DEV)
    label_blocks = labels.reshape(N_ROWS, ROW_DEV)

    def step(carry, items):
        g_sum, h_sum = block_terms(items[0], items[1], items[2])
        return (carry[0] + g_sum, carry[1] + h_sum), None

    start = (jnp.zeros((LEAVES, C), jnp.float32), jnp.zeros((LEAVES, C), jnp.float32))
    sums, _ = lax.scan(step, start, (blocks, leaf_blocks, label_blocks))
    leaf_values = -0.3 * sums[0] / (sums[1] + 1.0)

    def apply(items):
        leaves = jnp.arange(LEAVES, dtype=jnp.int32)[None, :]
        onehot = (items[1][:, None] == leaves).astype(jnp.float32)
        return items[0] + jnp.dot(onehot, leaf_values, precision=lax.Precision.HIGHEST, preferred_element_type=jnp.float32)

    updated = lax.map(apply, (blocks, leaf_blocks)).reshape(ROWS, C)
    return leaf_values, updated
```

```python
import functools

import jax
import jax.numpy as jnp
from jax import lax
from jax.experimental import pallas as pl
from jax.experimental.pallas import tpu as pltpu
from jax.sharding import PartitionSpec as P

LEAVES = 128
LANES = 128
MESH = pl.DeviceIdType.MESH
F32 = jnp.float32
BF16 = jnp.bfloat16
CHUNKS = 4


def split(value):
    high = value.astype(BF16)
    return high, (value - high.astype(F32)).astype(BF16)


def kernel(
    n_cls, n_y, n_z,
    x_hbm, leaf_ref, label_ref,
    lv_out, up_out,
    x_v, e_v, stats, onehot, terms, sums, y_in, z_out, z_in, lv_z, lv_y, lv_all,
    x_sem, up_sem, s_send, s_recv, yr_send, yr_recv, zr_send, zr_recv, za_send, za_recv, ya_send, ya_recv,
):
    row, cls = lax.axis_index("rows"), lax.axis_index("cls")
    z, y = row // n_y, row % n_y
    rows = x_v.shape[0]
    blocks = rows // LANES
    per_chunk = blocks // CHUNKS
    chunk_rows = rows // CHUNKS

    def cls_peer(d):
        return {"rows": row, "cls": lax.rem(cls + d, n_cls)}

    def y_peer(d):
        return {"rows": z * n_y + lax.rem(y + d, n_y), "cls": cls}

    def z_peer(d):
        return {"rows": lax.rem(z + d, n_z) * n_y + y, "cls": cls}

    loads = []
    for c in range(CHUNKS):
        part = pl.ds(c * chunk_rows, chunk_rows)
        load = pltpu.make_async_copy(x_hbm.at[part], x_v.at[part], x_sem.at[c])
        load.start()
        loads.append(load)

    barrier = pltpu.get_barrier_semaphore()
    for d in range(1, n_cls):
        pl.semaphore_signal(barrier, inc=1, device_id=cls_peer(d), device_id_type=MESH)
    for d in range(1, n_y):
        pl.semaphore_signal(barrier, inc=1, device_id=y_peer(d), device_id_type=MESH)
    for d in range(1, n_z):
        pl.semaphore_signal(barrier, inc=1, device_id=z_peer(d), device_id_type=MESH)

    exchanges = []
    for c in range(CHUNKS):
        loads[c].wait()

        def local(i, carry, c=c):
            at = pl.ds(pl.multiple_of((c * per_chunk + i) * LANES, LANES), LANES)
            xt = x_v[at, :].T
            peak = jnp.max(xt, axis=0, keepdims=True)
            expo = jnp.exp(xt - peak)
            e_v[:, at] = expo
            stats[0, c, 0, pl.ds(i, 1), :] = peak
            stats[0, c, 1, pl.ds(i, 1), :] = jnp.sum(expo, axis=0, keepdims=True)
            return carry

        lax.fori_loop(0, per_chunk, local, 0)
        if c == 0:
            pl.semaphore_wait(barrier, n_cls + n_y + n_z - 3)
        for d in range(1, n_cls):
            copy = pltpu.make_async_remote_copy(
                stats.at[0, c], stats.at[d, c], s_send.at[d, c], s_recv.at[d, c],
                device_id=cls_peer(d), device_id_type=MESH,
            )
            copy.start()
            exchanges.append(copy)

    def one_hot(i, carry):
        at = pl.ds(pl.multiple_of(i * LANES, LANES), LANES)
        which = lax.broadcasted_iota(jnp.int32, (LEAVES, LANES), 0)
        hot = (which == leaf_ref[pl.ds(i, 1), :]).astype(F32).T.astype(BF16)
        onehot[at, 0:LEAVES] = hot
        onehot[at, LEAVES : 2 * LEAVES] = hot
        return carry

    lax.fori_loop(0, blocks, one_hot, 0)

    width = e_v.shape[0]
    for c in range(CHUNKS):
        for d in range(1, n_cls):
            exchanges[c * (n_cls - 1) + d - 1].wait()
        peak = stats[0, c, 0]
        for d in range(1, n_cls):
            peak = jnp.maximum(peak, stats[d, c, 0])
        own = jnp.exp(stats[0, c, 0] - peak)
        total = stats[0, c, 1] * own
        for d in range(1, n_cls):
            total = total + stats[d, c, 1] * jnp.exp(stats[d, c, 0] - peak)
        stats[0, c, 1] = own / total

        def derive(i, carry, c=c):
            k = c * per_chunk + i
            at = pl.ds(pl.multiple_of(k * LANES, LANES), LANES)
            prob = e_v[:, at] * stats[0, c, 1, pl.ds(i, 1), :]
            classes = lax.broadcasted_iota(jnp.int32, (width, LANES), 0) + cls * width
            grad = prob - (classes == label_ref[pl.ds(k, 1), :]).astype(F32)
            hess = prob * (1.0 - prob)
            terms[0:width, at], terms[width : 2 * width, at] = split(grad)
            terms[2 * width : 3 * width, at], terms[3 * width : 4 * width, at] = split(hess)
            return carry

        lax.fori_loop(0, per_chunk, derive, 0)

    acc = jnp.dot(terms[...], onehot[:, 0:LEAVES], preferred_element_type=F32)
    sums[0] = acc[0:width] + acc[width : 2 * width]
    sums[1] = acc[2 * width : 3 * width] + acc[3 * width : 4 * width]

    quarter = width // n_y
    copies = []
    for d in range(1, n_y):
        theirs = pl.ds(pl.multiple_of(lax.rem(y + d, n_y) * quarter, quarter), quarter)
        copy = pltpu.make_async_remote_copy(
            sums.at[:, theirs], y_in.at[d - 1], yr_send.at[d], yr_recv.at[d],
            device_id=y_peer(d), device_id_type=MESH,
        )
        copy.start()
        copies.append(copy)
    mine = sums[:, pl.ds(pl.multiple_of(y * quarter, quarter), quarter), :]
    for d in range(1, n_y):
        copies[d - 1].wait()
        mine = mine + y_in[d - 1]

    few = quarter // n_z
    for k in range(n_z):
        z_out[k, 0] = mine[0, k * few : (k + 1) * few]
        z_out[k, 1] = mine[1, k * few : (k + 1) * few]
    copies = []
    for d in range(1, n_z):
        copy = pltpu.make_async_remote_copy(
            z_out.at[lax.rem(z + d, n_z)], z_in.at[d - 1], zr_send.at[d], zr_recv.at[d],
            device_id=z_peer(d), device_id_type=MESH,
        )
        copy.start()
        copies.append(copy)
    mine = z_out[z]
    for d in range(1, n_z):
        copies[d - 1].wait()
        mine = mine + z_in[d - 1]
    lv_z[z] = -0.3 * mine[0] / (mine[1] + 1.0)

    sends = []
    for d in range(1, n_z):
        copy = pltpu.make_async_remote_copy(
            lv_z.at[z], lv_z.at[z], za_send.at[d], za_recv.at[d],
            device_id=z_peer(d), device_id_type=MESH,
        )
        copy.start()
        sends.append(copy)
    for d in range(1, n_z):
        source = lax.rem(z + n_z - d, n_z)
        pltpu.make_async_remote_copy(
            lv_z.at[source], lv_z.at[source], za_send.at[d], za_recv.at[d],
            device_id=z_peer(d), device_id_type=MESH,
        ).wait_recv()
    for k in range(n_z):
        lv_y[y, k * few : (k + 1) * few] = lv_z[k]
    for d in range(1, n_y):
        copy = pltpu.make_async_remote_copy(
            lv_y.at[y], lv_y.at[y], ya_send.at[d], ya_recv.at[d],
            device_id=y_peer(d), device_id_type=MESH,
        )
        copy.start()
        sends.append(copy)
    for d in range(1, n_y):
        source = lax.rem(y + n_y - d, n_y)
        pltpu.make_async_remote_copy(
            lv_y.at[source], lv_y.at[source], ya_send.at[d], ya_recv.at[d],
            device_id=y_peer(d), device_id_type=MESH,
        ).wait_recv()

    leaf_values = lv_y[...].reshape(width, LEAVES).T
    lv_out[...] = leaf_values
    lv_all[0:LEAVES, :], lv_all[LEAVES : 2 * LEAVES, :] = split(leaf_values)

    def update(i, carry):
        at = pl.ds(pl.multiple_of(i * 256, 256), 256)
        up_out[at, :] = x_v[at, :] + jnp.dot(onehot[at, :], lv_all[...], preferred_element_type=F32)
        return carry

    lax.fori_loop(0, rows // 256, update, 0)
    for copy in sends:
        copy.wait_send()


def solution(mesh):
    n_cls, n_rows = mesh.shape["cls"], mesh.shape["rows"]
    n_y = 4
    n_z = n_rows // n_y

    def per_device(logits, leaf_index, labels):
        rows, width = logits.shape
        blocks = rows // LANES
        quarter = width // n_y
        few = quarter // n_z
        dma = pltpu.SemaphoreType.DMA
        vmem = pl.BlockSpec(memory_space=pltpu.VMEM)
        return pl.pallas_call(
            functools.partial(kernel, n_cls, n_y, n_z),
            out_shape=(
                jax.ShapeDtypeStruct((LEAVES, width), F32),
                jax.ShapeDtypeStruct((rows, width), F32),
            ),
            in_specs=[pl.BlockSpec(memory_space=pltpu.HBM), vmem, vmem],
            out_specs=(vmem, vmem),
            scratch_shapes=[
                pltpu.VMEM((rows, width), F32),
                pltpu.VMEM((width, rows), F32),
                pltpu.VMEM((n_cls, CHUNKS, 2, blocks // CHUNKS, LANES), F32),
                pltpu.VMEM((rows, 2 * LEAVES), BF16),
                pltpu.VMEM((4 * width, rows), BF16),
                pltpu.VMEM((2, width, LEAVES), F32),
                pltpu.VMEM((n_y - 1, 2, quarter, LEAVES), F32),
                pltpu.VMEM((n_z, 2, few, LEAVES), F32),
                pltpu.VMEM((n_z - 1, 2, few, LEAVES), F32),
                pltpu.VMEM((n_z, few, LEAVES), F32),
                pltpu.VMEM((n_y, quarter, LEAVES), F32),
                pltpu.VMEM((2 * LEAVES, width), BF16),
                dma((CHUNKS,)),
                dma((CHUNKS,)),
                dma((n_cls, CHUNKS)),
                dma((n_cls, CHUNKS)),
                dma((n_y,)),
                dma((n_y,)),
                dma((n_z,)),
                dma((n_z,)),
                dma((n_z,)),
                dma((n_z,)),
                dma((n_y,)),
                dma((n_y,)),
            ],
            compiler_params=pltpu.CompilerParams(
                collective_id=0, has_side_effects=True, vmem_limit_bytes=32 * 2**20
            ),
        )(logits, leaf_index.reshape(blocks, LANES), labels.reshape(blocks, LANES))

    return jax.shard_map(
        per_device,
        mesh=mesh,
        in_specs=(P("rows", "cls"), P("rows"), P("rows")),
        out_specs=(P(None, "cls"), P("rows", "cls")),
        check_vma=False,
    )
```

```python
import functools

import jax
import jax.numpy as jnp
from jax import lax
from jax.experimental import pallas as pl
from jax.experimental.pallas import tpu as pltpu
from jax.sharding import PartitionSpec as P

LEAVES = 128
LANES = 128
MESH = pl.DeviceIdType.MESH
F32 = jnp.float32
BF16 = jnp.bfloat16
CHUNKS = 4


def in_hbm(array):
    return pltpu.with_memory_space_constraint(array, pltpu.HBM)


def split(value):
    high = value.astype(BF16)
    return high, (value - high.astype(F32)).astype(BF16)


def kernel(
    n_cls, n_y, n_z,
    x_hbm, leaf_hbm, label_hbm,
    lv_out, x_v, onehot,
    leaf_v, label_v, e_v, stats, onehot_t, terms, sums, near, far, lv_t,
    load_sem, s_send, s_recv, r_send, r_recv, f_send, f_recv, g_send, g_recv,
):
    row, cls = lax.axis_index("rows"), lax.axis_index("cls")
    z, y = row // n_y, row % n_y
    half, odd = z // 2, z % 2
    n_half = n_z // 2
    rows, width = x_v.shape
    blocks = rows // LANES
    per_chunk = blocks // CHUNKS
    chunk_rows = rows // CHUNKS

    def cls_peer(d):
        return {"rows": row, "cls": lax.rem(cls + d, n_cls)}

    def near_place(j):
        dy, flip = j // 2, j % 2
        return lax.rem(y + dy, n_y), (1 - odd if flip else odd)

    def near_peer(j):
        to_y, to_odd = near_place(j)
        return {"rows": (half * 2 + to_odd) * n_y + to_y, "cls": cls}

    def far_peer(d):
        return {"rows": (lax.rem(half + d, n_half) * 2 + odd) * n_y + y, "cls": cls}

    loads = []
    for c in range(CHUNKS):
        part = pl.ds(c * chunk_rows, chunk_rows)
        loads.append(pltpu.make_async_copy(x_hbm.at[part], x_v.at[part], load_sem.at[c]))
    loads.append(pltpu.make_async_copy(leaf_hbm, leaf_v, load_sem.at[CHUNKS]))
    loads.append(pltpu.make_async_copy(label_hbm, label_v, load_sem.at[CHUNKS + 1]))
    for load in loads:
        load.start()

    barrier = pltpu.get_barrier_semaphore()
    for d in range(1, n_cls):
        pl.semaphore_signal(barrier, inc=1, device_id=cls_peer(d), device_id_type=MESH)
    for j in range(1, 2 * n_y):
        pl.semaphore_signal(barrier, inc=1, device_id=near_peer(j), device_id_type=MESH)
    for d in range(1, n_half):
        pl.semaphore_signal(barrier, inc=1, device_id=far_peer(d), device_id_type=MESH)

    exchanges = []
    for c in range(CHUNKS):
        loads[c].wait()

        def local(i, carry, c=c):
            at = pl.ds(pl.multiple_of((c * per_chunk + i) * LANES, LANES), LANES)
            xt = x_v[at, :].T
            peak = jnp.max(xt, axis=0, keepdims=True)
            expo = jnp.exp(xt - peak)
            e_v[:, at] = expo
            stats[0, c, 0, pl.ds(i, 1), :] = peak
            stats[0, c, 1, pl.ds(i, 1), :] = jnp.sum(expo, axis=0, keepdims=True)
            return carry

        lax.fori_loop(0, per_chunk, local, 0, unroll=4)
        if c == 0:
            pl.semaphore_wait(barrier, n_cls + 2 * n_y + n_half - 3)
        for d in range(1, n_cls):
            copy = pltpu.make_async_remote_copy(
                stats.at[0, c], stats.at[d, c], s_send.at[d, c], s_recv.at[d, c],
                device_id=cls_peer(d), device_id_type=MESH,
            )
            copy.start()
            exchanges.append(copy)

    loads[CHUNKS].wait()
    loads[CHUNKS + 1].wait()

    def one_hot_t(i, carry):
        at = pl.ds(pl.multiple_of(i * LANES, LANES), LANES)
        which = lax.broadcasted_iota(jnp.int32, (LEAVES, LANES), 0)
        onehot_t[:, at] = (which == leaf_v[pl.ds(i, 1), :]).astype(F32).astype(BF16)
        return carry

    lax.fori_loop(0, blocks, one_hot_t, 0, unroll=4)

    for c in range(CHUNKS):
        for d in range(1, n_cls):
            exchanges[c * (n_cls - 1) + d - 1].wait()
        peak = stats[0, c, 0]
        for d in range(1, n_cls):
            peak = jnp.maximum(peak, stats[d, c, 0])
        own = jnp.exp(stats[0, c, 0] - peak)
        total = stats[0, c, 1] * own
        for d in range(1, n_cls):
            total = total + stats[d, c, 1] * jnp.exp(stats[d, c, 0] - peak)
        stats[0, c, 1] = own / total

        def derive(i, carry, c=c):
            k = c * per_chunk + i
            at = pl.ds(pl.multiple_of(k * LANES, LANES), LANES)
            prob = e_v[:, at] * stats[0, c, 1, pl.ds(i, 1), :]
            classes = lax.broadcasted_iota(jnp.int32, (width, LANES), 0) + cls * width
            grad = prob - (classes == label_v[pl.ds(k, 1), :]).astype(F32)
            hess = prob * (1.0 - prob)
            terms[0:width, at], terms[width : 2 * width, at] = split(grad)
            terms[2 * width : 3 * width, at], terms[3 * width : 4 * width, at] = split(hess)
            return carry

        lax.fori_loop(0, per_chunk, derive, 0, unroll=4)

    acc = lax.dot_general(
        terms[...], onehot_t[...], (((1,), (1,)), ((), ())), preferred_element_type=F32
    )
    sums[0] = acc[0:width] + acc[width : 2 * width]
    sums[1] = acc[2 * width : 3 * width] + acc[3 * width : 4 * width]

    piece = width // (2 * n_y)
    copies = []
    for j in range(1, 2 * n_y):
        to_y, to_odd = near_place(j)
        theirs = pl.ds(pl.multiple_of((to_y * 2 + to_odd) * piece, piece), piece)
        copy = pltpu.make_async_remote_copy(
            sums.at[:, theirs], near.at[j], r_send.at[j], r_recv.at[j],
            device_id=near_peer(j), device_id_type=MESH,
        )
        copy.start()
        copies.append(copy)
    mine = y * 2 + odd
    total = sums[:, pl.ds(pl.multiple_of(mine * piece, piece), piece), :]
    for j in range(1, 2 * n_y):
        copies[j - 1].wait()
        total = total + near[j]
    far[half] = total

    copies = []
    for d in sorted(range(1, n_half), key=lambda d: abs(n_half - 2 * d)):
        copy = pltpu.make_async_remote_copy(
            far.at[half], far.at[half], f_send.at[d], f_recv.at[d],
            device_id=far_peer(d), device_id_type=MESH,
        )
        copy.start()
        copies.append(copy)

    def one_hot(i, carry):
        at = pl.ds(pl.multiple_of(i * LANES, LANES), LANES)
        hot = onehot_t[:, at].T
        onehot[at, 0:LEAVES] = hot
        onehot[at, LEAVES : 2 * LEAVES] = hot
        return carry

    lax.fori_loop(0, blocks, one_hot, 0, unroll=2)

    for d in range(1, n_half):
        source = lax.rem(half + n_half - d, n_half)
        pltpu.make_async_remote_copy(
            far.at[source], far.at[source], f_send.at[d], f_recv.at[d],
            device_id=far_peer(d), device_id_type=MESH,
        ).wait_recv()
    total = far[0]
    for k in range(1, n_half):
        total = total + far[k]
    lv_t[mine] = -0.3 * total[0] / (total[1] + 1.0)

    for j in range(1, 2 * n_y):
        copy = pltpu.make_async_remote_copy(
            lv_t.at[mine], lv_t.at[mine], g_send.at[j], g_recv.at[j],
            device_id=near_peer(j), device_id_type=MESH,
        )
        copy.start()
        copies.append(copy)
    for j in range(1, 2 * n_y):
        dy, flip = j // 2, j % 2
        source = lax.rem(y + n_y - dy, n_y) * 2 + (1 - odd if flip else odd)
        pltpu.make_async_remote_copy(
            lv_t.at[source], lv_t.at[source], g_send.at[j], g_recv.at[j],
            device_id=near_peer(j), device_id_type=MESH,
        ).wait_recv()
    lv_out[...] = lv_t[...].reshape(width, LEAVES).T
    for copy in copies:
        copy.wait_send()


def update(x_v, onehot, lv, lv_hbm, up_hbm, up_v, sem):
    values = jnp.concatenate(split(lv[...]), axis=0)
    copies = [pltpu.make_async_copy(lv, lv_hbm, sem.at[CHUNKS])]
    copies[0].start()
    chunk_rows = x_v.shape[0] // CHUNKS
    for c in range(CHUNKS):
        def part(i, carry, c=c):
            at = pl.ds(pl.multiple_of(c * chunk_rows + i * 256, 256), 256)
            up_v[at, :] = x_v[at, :] + jnp.dot(onehot[at, :], values, preferred_element_type=F32)
            return carry

        lax.fori_loop(0, chunk_rows // 256, part, 0, unroll=2)
        at = pl.ds(c * chunk_rows, chunk_rows)
        copies.append(pltpu.make_async_copy(up_v.at[at], up_hbm.at[at], sem.at[c]))
        copies[-1].start()
    for copy in copies:
        copy.wait()


def solution(mesh):
    n_cls, n_rows = mesh.shape["cls"], mesh.shape["rows"]
    n_y = 4
    n_z = n_rows // n_y

    def per_device(logits, leaf_index, labels):
        rows, width = logits.shape
        blocks = rows // LANES
        piece = width // (2 * n_y)
        dma = pltpu.SemaphoreType.DMA
        vmem = pl.BlockSpec(memory_space=pltpu.VMEM)
        hbm = pl.BlockSpec(memory_space=pltpu.HBM)
        leaf_values, x_v, onehot = pl.pallas_call(
            functools.partial(kernel, n_cls, n_y, n_z),
            out_shape=(
                pltpu.VMEM((LEAVES, width), F32),
                pltpu.VMEM((rows, width), F32),
                pltpu.VMEM((rows, 2 * LEAVES), BF16),
            ),
            in_specs=[hbm, hbm, hbm],
            out_specs=(vmem, vmem, vmem),
            scratch_shapes=[
                pltpu.VMEM((blocks, LANES), jnp.int32),
                pltpu.VMEM((blocks, LANES), jnp.int32),
                pltpu.VMEM((width, rows), F32),
                pltpu.VMEM((n_cls, CHUNKS, 2, blocks // CHUNKS, LANES), F32),
                pltpu.VMEM((LEAVES, rows), BF16),
                pltpu.VMEM((4 * width, rows), BF16),
                pltpu.VMEM((2, width, LEAVES), F32),
                pltpu.VMEM((2 * n_y, 2, piece, LEAVES), F32),
                pltpu.VMEM((n_z // 2, 2, piece, LEAVES), F32),
                pltpu.VMEM((2 * n_y, piece, LEAVES), F32),
                dma((CHUNKS + 2,)),
                dma((n_cls, CHUNKS)),
                dma((n_cls, CHUNKS)),
                dma((2 * n_y,)),
                dma((2 * n_y,)),
                dma((n_z // 2,)),
                dma((n_z // 2,)),
                dma((2 * n_y,)),
                dma((2 * n_y,)),
            ],
            compiler_params=pltpu.CompilerParams(
                collective_id=0, has_side_effects=True, vmem_limit_bytes=32 * 2**20
            ),
        )(
            in_hbm(logits),
            in_hbm(leaf_index.reshape(blocks, LANES)),
            in_hbm(labels.reshape(blocks, LANES)),
        )
        return pl.pallas_call(
            update,
            out_shape=(
                pltpu.HBM((LEAVES, width), F32),
                pltpu.HBM((rows, width), F32),
            ),
            in_specs=[vmem, vmem, vmem],
            out_specs=(hbm, hbm),
            scratch_shapes=[pltpu.VMEM((rows, width), F32), dma((CHUNKS + 1,))],
            compiler_params=pltpu.CompilerParams(vmem_limit_bytes=16 * 2**20),
        )(x_v, onehot, leaf_values)

    return jax.shard_map(
        per_device,
        mesh=mesh,
        in_specs=(P("rows", "cls"), P("rows"), P("rows")),
        out_specs=(P(None, "cls"), P("rows", "cls")),
        check_vma=False,
    )
```

```python
import functools

import jax
import jax.numpy as jnp
from jax import lax
from jax.experimental import pallas as pl
from jax.experimental.pallas import tpu as pltpu
from jax.sharding import PartitionSpec as P

LEAVES = 128
LANES = 128
MESH = pl.DeviceIdType.MESH
F32 = jnp.float32
BF16 = jnp.bfloat16
CHUNKS = 4
PARTS = 2
WRITES = 8


def in_hbm(array):
    return pltpu.with_memory_space_constraint(array, pltpu.HBM)


def split(value):
    high = value.astype(BF16)
    return high, (value - high.astype(F32)).astype(BF16)


def kernel(
    n_cls, n_y, n_z,
    x_hbm, leaf_hbm, label_hbm,
    lv_out, x_v, onehot,
    leaf_v, label_v, e_v, stats, chip, onehot_t, terms, sums, near, far, lv_t,
    load_sem, c_send, c_recv, s_send, s_recv, r_send, r_recv, f_send, f_recv, g_send, g_recv,
):
    row, cls = lax.axis_index("rows"), lax.axis_index("cls")
    z, y = row // n_y, row % n_y
    half, odd = z // 2, z % 2
    n_half = n_z // 2
    rows, width = x_v.shape
    blocks = rows // LANES
    per_chunk = blocks // CHUNKS
    chunk_rows = rows // CHUNKS

    core = cls % 2
    n_x = n_cls // 2

    def core_peer():
        return {"rows": row, "cls": cls + 1 - 2 * core}

    def x_peer(d):
        return {"rows": row, "cls": lax.rem(cls + 2 * d, n_cls)}

    def near_place(j):
        dy, flip = j // 2, j % 2
        return lax.rem(y + dy, n_y), (1 - odd if flip else odd)

    def near_peer(j):
        to_y, to_odd = near_place(j)
        return {"rows": (half * 2 + to_odd) * n_y + to_y, "cls": cls}

    def far_peer(d):
        return {"rows": (lax.rem(half + d, n_half) * 2 + odd) * n_y + y, "cls": cls}

    loads = []
    for c in range(CHUNKS):
        part = pl.ds(c * chunk_rows, chunk_rows)
        loads.append(pltpu.make_async_copy(x_hbm.at[part], x_v.at[part], load_sem.at[c]))
    loads.append(pltpu.make_async_copy(leaf_hbm, leaf_v, load_sem.at[CHUNKS]))
    loads.append(pltpu.make_async_copy(label_hbm, label_v, load_sem.at[CHUNKS + 1]))
    for load in loads:
        load.start()

    barrier = pltpu.get_barrier_semaphore()
    for d in range(1, n_x):
        pl.semaphore_signal(barrier, inc=1, device_id=x_peer(d), device_id_type=MESH)
    pl.semaphore_signal(barrier, inc=1, device_id=core_peer(), device_id_type=MESH)
    for d in range(1, n_half):
        pl.semaphore_signal(barrier, inc=1, device_id=far_peer(d), device_id_type=MESH)
    for j in range(1, 2 * n_y):
        pl.semaphore_signal(barrier, inc=1, device_id=near_peer(j), device_id_type=MESH)

    per_part = blocks // PARTS
    for c in range(CHUNKS):
        loads[c].wait()

        def local(i, carry, c=c):
            k = c * per_chunk + i
            at = pl.ds(pl.multiple_of(k * LANES, LANES), LANES)
            xt = x_v[at, :].T
            peak = jnp.max(xt, axis=0, keepdims=True)
            expo = jnp.exp(xt - peak)
            e_v[:, at] = expo
            h = c * per_chunk // per_part
            at = pl.ds(k - h * per_part, 1)
            stats[0, h, 0, at, :] = peak
            stats[0, h, 1, at, :] = jnp.sum(expo, axis=0, keepdims=True)
            return carry

        lax.fori_loop(0, per_chunk, local, 0, unroll=8)

    loads[CHUNKS].wait()
    loads[CHUNKS + 1].wait()

    def one_hot_t(i, carry):
        at = pl.ds(pl.multiple_of(i * LANES, LANES), LANES)
        which = lax.broadcasted_iota(jnp.int32, (LEAVES, LANES), 0)
        onehot_t[:, at] = (which == leaf_v[pl.ds(i, 1), :]).astype(F32).astype(BF16)
        return carry

    lax.fori_loop(0, blocks, one_hot_t, 0, unroll=4)

    pl.semaphore_wait(barrier, n_x + 2 * n_y + n_half - 2)
    swaps = []
    for h in range(PARTS):
        copy = pltpu.make_async_remote_copy(
            stats.at[0, h], stats.at[1, h], c_send.at[h], c_recv.at[h],
            device_id=core_peer(), device_id_type=MESH,
        )
        copy.start()
        swaps.append(copy)
    exchanges = []
    for h in range(PARTS):
        swaps[h].wait()
        peak = jnp.maximum(stats[0, h, 0], stats[1, h, 0])
        chip[0, h, 0] = peak
        chip[0, h, 1] = (
            stats[0, h, 1] * jnp.exp(stats[0, h, 0] - peak)
            + stats[1, h, 1] * jnp.exp(stats[1, h, 0] - peak)
        )
        for d in range(1, n_x):
            copy = pltpu.make_async_remote_copy(
                chip.at[0, h], chip.at[d, h], s_send.at[d, h], s_recv.at[d, h],
                device_id=x_peer(d), device_id_type=MESH,
            )
            copy.start()
            exchanges.append(copy)

    piece = width // (2 * n_y)

    def share(g):
        copies = []
        for j in near_order:
            to_y, to_odd = near_place(j)
            theirs = pl.ds(pl.multiple_of((to_y * 2 + to_odd) * piece, piece), piece)
            copy = pltpu.make_async_remote_copy(
                sums.at[g, theirs], near.at[j, g], r_send.at[j, g], r_recv.at[j, g],
                device_id=near_peer(j), device_id_type=MESH,
            )
            copy.start()
            copies.append(copy)
        return copies

    near_order = sorted(range(1, 2 * n_y), key=lambda j: -(min(j // 2, n_y - j // 2) + j % 2))
    shares = []
    for h in range(PARTS):
        for d in range(1, n_x):
            exchanges[h * (n_x - 1) + d - 1].wait()
        peak = chip[0, h, 0]
        for d in range(1, n_x):
            peak = jnp.maximum(peak, chip[d, h, 0])
        total = chip[0, h, 1] * jnp.exp(chip[0, h, 0] - peak)
        for d in range(1, n_x):
            total = total + chip[d, h, 1] * jnp.exp(chip[d, h, 0] - peak)
        stats[0, h, 1] = jnp.exp(stats[0, h, 0] - peak) / total

        def derive(i, carry, h=h):
            k = h * per_part + i
            at = pl.ds(pl.multiple_of(k * LANES, LANES), LANES)
            prob = e_v[:, at] * stats[0, h, 1, pl.ds(i, 1), :]
            classes = lax.broadcasted_iota(jnp.int32, (width, LANES), 0) + cls * width
            grad = prob - (classes == label_v[pl.ds(k, 1), :]).astype(F32)
            hess = prob * (1.0 - prob)
            terms[0:width, at], terms[width : 2 * width, at] = split(grad)
            terms[2 * width : 3 * width, at], terms[3 * width : 4 * width, at] = split(hess)
            return carry

        lax.fori_loop(0, per_part, derive, 0, unroll=4)

        part = slice(h * per_part * LANES, (h + 1) * per_part * LANES)
        for g in range(2):
            acc = lax.dot_general(
                terms[2 * g * width : 2 * (g + 1) * width, part],
                onehot_t[:, part],
                (((1,), (1,)), ((), ())),
                preferred_element_type=F32,
            )
            acc = acc[0:width] + acc[width : 2 * width]
            sums[g] = acc if h == 0 else sums[g] + acc
            if h == PARTS - 1:
                shares.append(share(g))

    mine = y * 2 + odd
    own_part = pl.ds(pl.multiple_of(mine * piece, piece), piece)
    for g in range(2):
        for copy in shares[g]:
            copy.wait()
        total = sums[g, own_part, :]
        for j in range(1, 2 * n_y):
            total = total + near[j, g]
        far[half, g] = total

    copies = []
    for k in range(n_half - 1):
        to = jnp.where(half <= k, k + 1, k)
        copy = pltpu.make_async_remote_copy(
            far.at[half], far.at[half], f_send.at[k], f_recv.at[half],
            device_id={"rows": (to * 2 + odd) * n_y + y, "cls": cls}, device_id_type=MESH,
        )
        copy.start()
        copies.append(copy)

    def one_hot(i, carry):
        at = pl.ds(pl.multiple_of(i * LANES, LANES), LANES)
        hot = onehot_t[:, at].T
        onehot[at, 0:LEAVES] = hot
        onehot[at, LEAVES : 2 * LEAVES] = hot
        return carry

    lax.fori_loop(0, blocks, one_hot, 0, unroll=8)

    for d in range(1, n_half):
        source = lax.rem(half + n_half - d, n_half)
        pltpu.make_async_remote_copy(
            far.at[source], far.at[source], f_send.at[d], f_recv.at[source],
            device_id=far_peer(d), device_id_type=MESH,
        ).wait_recv()
    total = far[0]
    for k in range(1, n_half):
        total = total + far[k]
    lv_t[mine] = -0.3 * total[0] / (total[1] + 1.0)

    for j in near_order:
        copy = pltpu.make_async_remote_copy(
            lv_t.at[mine], lv_t.at[mine], g_send.at[j], g_recv.at[j],
            device_id=near_peer(j), device_id_type=MESH,
        )
        copy.start()
        copies.append(copy)
    for j in range(1, 2 * n_y):
        dy, flip = j // 2, j % 2
        source = lax.rem(y + n_y - dy, n_y) * 2 + (1 - odd if flip else odd)
        pltpu.make_async_remote_copy(
            lv_t.at[source], lv_t.at[source], g_send.at[j], g_recv.at[j],
            device_id=near_peer(j), device_id_type=MESH,
        ).wait_recv()
    lv_out[...] = lv_t[...].reshape(width, LEAVES).T
    for copy in copies:
        copy.wait_send()


def update(x_v, onehot, lv, lv_hbm, up_hbm, up_v, sem):
    values = jnp.concatenate(split(lv[...]), axis=0)
    copies = [pltpu.make_async_copy(lv, lv_hbm, sem.at[WRITES])]
    copies[0].start()
    chunk_rows = x_v.shape[0] // WRITES
    for c in range(WRITES):
        def part(i, carry, c=c):
            at = pl.ds(pl.multiple_of(c * chunk_rows + i * 256, 256), 256)
            up_v[at, :] = x_v[at, :] + jnp.dot(onehot[at, :], values, preferred_element_type=F32)
            return carry

        lax.fori_loop(0, chunk_rows // 256, part, 0, unroll=2)
        at = pl.ds(c * chunk_rows, chunk_rows)
        copies.append(pltpu.make_async_copy(up_v.at[at], up_hbm.at[at], sem.at[c]))
        copies[-1].start()
    for copy in copies:
        copy.wait()


def solution(mesh):
    n_cls, n_rows = mesh.shape["cls"], mesh.shape["rows"]
    n_y = 4
    n_z = n_rows // n_y

    def per_device(logits, leaf_index, labels):
        rows, width = logits.shape
        blocks = rows // LANES
        piece = width // (2 * n_y)
        dma = pltpu.SemaphoreType.DMA
        vmem = pl.BlockSpec(memory_space=pltpu.VMEM)
        hbm = pl.BlockSpec(memory_space=pltpu.HBM)
        leaf_values, x_v, onehot = pl.pallas_call(
            functools.partial(kernel, n_cls, n_y, n_z),
            out_shape=(
                pltpu.VMEM((LEAVES, width), F32),
                pltpu.VMEM((rows, width), F32),
                pltpu.VMEM((rows, 2 * LEAVES), BF16),
            ),
            in_specs=[hbm, hbm, hbm],
            out_specs=(vmem, vmem, vmem),
            scratch_shapes=[
                pltpu.VMEM((blocks, LANES), jnp.int32),
                pltpu.VMEM((blocks, LANES), jnp.int32),
                pltpu.VMEM((width, rows), F32),
                pltpu.VMEM((2, PARTS, 2, blocks // PARTS, LANES), F32),
                pltpu.VMEM((n_cls // 2, PARTS, 2, blocks // PARTS, LANES), F32),
                pltpu.VMEM((LEAVES, rows), BF16),
                pltpu.VMEM((4 * width, rows), BF16),
                pltpu.VMEM((2, width, LEAVES), F32),
                pltpu.VMEM((2 * n_y, 2, piece, LEAVES), F32),
                pltpu.VMEM((n_z // 2, 2, piece, LEAVES), F32),
                pltpu.VMEM((2 * n_y, piece, LEAVES), F32),
                dma((CHUNKS + 2,)),
                dma((PARTS,)),
                dma((PARTS,)),
                dma((n_cls // 2, PARTS)),
                dma((n_cls // 2, PARTS)),
                dma((2 * n_y, 2)),
                dma((2 * n_y, 2)),
                dma((n_z // 2,)),
                dma((n_z // 2,)),
                dma((2 * n_y,)),
                dma((2 * n_y,)),
            ],
            compiler_params=pltpu.CompilerParams(
                collective_id=0, has_side_effects=True, vmem_limit_bytes=32 * 2**20
            ),
        )(
            in_hbm(logits),
            in_hbm(leaf_index.reshape(blocks, LANES)),
            in_hbm(labels.reshape(blocks, LANES)),
        )
        return pl.pallas_call(
            update,
            out_shape=(
                pltpu.HBM((LEAVES, width), F32),
                pltpu.HBM((rows, width), F32),
            ),
            in_specs=[vmem, vmem, vmem],
            out_specs=(hbm, hbm),
            scratch_shapes=[pltpu.VMEM((rows, width), F32), dma((WRITES + 1,))],
            compiler_params=pltpu.CompilerParams(vmem_limit_bytes=16 * 2**20),
        )(x_v, onehot, leaf_values)

    return jax.shard_map(
        per_device,
        mesh=mesh,
        in_specs=(P("rows", "cls"), P("rows"), P("rows")),
        out_specs=(P(None, "cls"), P("rows", "cls")),
        check_vma=False,
    )
```

```python
import functools

import jax
import jax.numpy as jnp
from jax import lax
from jax.experimental import pallas as pl
from jax.experimental.pallas import tpu as pltpu
from jax.sharding import PartitionSpec as P

LEAVES = 128
LANES = 128
MESH = pl.DeviceIdType.MESH
F32 = jnp.float32
BF16 = jnp.bfloat16
CHUNKS = 4
PARTS = 2
TOGETHER = 4
WRITES = 8


def in_hbm(array):
    return pltpu.with_memory_space_constraint(array, pltpu.HBM)


def split(value):
    high = value.astype(BF16)
    return high, (value - high.astype(F32)).astype(BF16)


def kernel(
    n_cls, n_y, n_z,
    x_hbm, leaf_hbm, label_hbm,
    lv_out, x_v, onehot,
    leaf_v, label_v, e_v, stats, chip, onehot_t, sums, near, far, lv_t,
    load_sem, c_send, c_recv, s_send, s_recv, r_send, r_recv, f_send, f_recv, g_send, g_recv,
):
    row, cls = lax.axis_index("rows"), lax.axis_index("cls")
    z, y = row // n_y, row % n_y
    half, odd = z // 2, z % 2
    n_half = n_z // 2
    rows, width = x_v.shape
    blocks = rows // LANES
    per_chunk = blocks // CHUNKS
    chunk_rows = rows // CHUNKS

    core = cls % 2
    n_x = n_cls // 2

    def core_peer():
        return {"rows": row, "cls": cls + 1 - 2 * core}

    def x_peer(d):
        return {"rows": row, "cls": lax.rem(cls + 2 * d, n_cls)}

    def near_place(j):
        dy, flip = j // 2, j % 2
        return lax.rem(y + dy, n_y), (1 - odd if flip else odd)

    def near_peer(j):
        to_y, to_odd = near_place(j)
        return {"rows": (half * 2 + to_odd) * n_y + to_y, "cls": cls}

    def far_peer(d):
        return {"rows": (lax.rem(half + d, n_half) * 2 + odd) * n_y + y, "cls": cls}

    loads = []
    for c in range(CHUNKS):
        part = pl.ds(c * chunk_rows, chunk_rows)
        loads.append(pltpu.make_async_copy(x_hbm.at[part], x_v.at[part], load_sem.at[c]))
    loads.append(pltpu.make_async_copy(leaf_hbm, leaf_v, load_sem.at[CHUNKS]))
    loads.append(pltpu.make_async_copy(label_hbm, label_v, load_sem.at[CHUNKS + 1]))
    for load in loads:
        load.start()

    barrier = pltpu.get_barrier_semaphore()
    for d in range(1, n_x):
        pl.semaphore_signal(barrier, inc=1, device_id=x_peer(d), device_id_type=MESH)
    pl.semaphore_signal(barrier, inc=1, device_id=core_peer(), device_id_type=MESH)
    for d in range(1, n_half):
        pl.semaphore_signal(barrier, inc=1, device_id=far_peer(d), device_id_type=MESH)
    for j in range(1, 2 * n_y):
        pl.semaphore_signal(barrier, inc=1, device_id=near_peer(j), device_id_type=MESH)

    per_part = blocks // PARTS
    for c in range(CHUNKS):
        loads[c].wait()

        def local(i, carry, c=c):
            k = c * per_chunk + i
            at = pl.ds(pl.multiple_of(k * LANES, LANES), LANES)
            xt = x_v[at, :].T
            peak = jnp.max(xt, axis=0, keepdims=True)
            expo = jnp.exp(xt - peak)
            e_v[:, at] = expo
            h = c * per_chunk // per_part
            at = pl.ds(k - h * per_part, 1)
            stats[0, h, 0, at, :] = peak
            stats[0, h, 1, at, :] = jnp.sum(expo, axis=0, keepdims=True)
            return carry

        lax.fori_loop(0, per_chunk, local, 0, unroll=8)

    pl.semaphore_wait(barrier, n_x + 2 * n_y + n_half - 2)
    swaps = []
    for h in range(PARTS):
        copy = pltpu.make_async_remote_copy(
            stats.at[0, h], stats.at[1, h], c_send.at[h], c_recv.at[h],
            device_id=core_peer(), device_id_type=MESH,
        )
        copy.start()
        swaps.append(copy)
    exchanges = []
    for h in range(PARTS):
        swaps[h].wait()
        peak = jnp.maximum(stats[0, h, 0], stats[1, h, 0])
        chip[0, h, 0] = peak
        chip[0, h, 1] = (
            stats[0, h, 1] * jnp.exp(stats[0, h, 0] - peak)
            + stats[1, h, 1] * jnp.exp(stats[1, h, 0] - peak)
        )
        for d in range(1, n_x):
            copy = pltpu.make_async_remote_copy(
                chip.at[0, h], chip.at[d, h], s_send.at[d, h], s_recv.at[d, h],
                device_id=x_peer(d), device_id_type=MESH,
            )
            copy.start()
            exchanges.append(copy)

    loads[CHUNKS].wait()
    loads[CHUNKS + 1].wait()

    def one_hot_t(i, carry):
        at = pl.ds(pl.multiple_of(i * LANES, LANES), LANES)
        which = lax.broadcasted_iota(jnp.int32, (LEAVES, LANES), 0)
        onehot_t[:, at] = (which == leaf_v[pl.ds(i, 1), :]).astype(F32).astype(BF16)
        return carry

    lax.fori_loop(0, blocks, one_hot_t, 0, unroll=4)

    piece = width // (2 * n_y)

    near_order = sorted(range(1, 2 * n_y), key=lambda j: -(min(j // 2, n_y - j // 2) + j % 2))
    classes = lax.broadcasted_iota(jnp.int32, (width, LANES), 0) + cls * width
    acc = None
    for h in range(PARTS):
        for d in range(1, n_x):
            exchanges[h * (n_x - 1) + d - 1].wait()
        peak = chip[0, h, 0]
        for d in range(1, n_x):
            peak = jnp.maximum(peak, chip[d, h, 0])
        total = chip[0, h, 1] * jnp.exp(chip[0, h, 0] - peak)
        for d in range(1, n_x):
            total = total + chip[d, h, 1] * jnp.exp(chip[d, h, 0] - peak)
        stats[0, h, 1] = jnp.exp(stats[0, h, 0] - peak) / total

        for k in range(h * per_part, (h + 1) * per_part, TOGETHER):
            grads, hessians = [], []
            for i in range(k, k + TOGETHER):
                at = slice(i * LANES, (i + 1) * LANES)
                inverse = i - h * per_part
                prob = e_v[:, at] * stats[0, h, 1, inverse : inverse + 1, :]
                grads.append(prob - (classes == label_v[i : i + 1, :]).astype(F32))
                hessians.append(prob * (1.0 - prob))
            at = slice(k * LANES, (k + TOGETHER) * LANES)
            terms = split(jnp.concatenate(grads, axis=1)) + split(jnp.concatenate(hessians, axis=1))
            part = lax.dot_general(
                jnp.concatenate(terms, axis=0), onehot_t[:, at],
                (((1,), (1,)), ((), ())), preferred_element_type=F32,
            )
            acc = part if acc is None else acc + part
    sums[0] = acc[0:width] + acc[width : 2 * width]
    sums[1] = acc[2 * width : 3 * width] + acc[3 * width : 4 * width]

    shares = []
    for j in near_order:
        to_y, to_odd = near_place(j)
        theirs = pl.ds(pl.multiple_of((to_y * 2 + to_odd) * piece, piece), piece)
        copy = pltpu.make_async_remote_copy(
            sums.at[:, theirs], near.at[j], r_send.at[j], r_recv.at[j],
            device_id=near_peer(j), device_id_type=MESH,
        )
        copy.start()
        shares.append(copy)

    mine = y * 2 + odd
    own_part = pl.ds(pl.multiple_of(mine * piece, piece), piece)
    for copy in shares:
        copy.wait()
    total = sums[:, own_part, :]
    for j in range(1, 2 * n_y):
        total = total + near[j]
    far[half] = total

    copies = []
    for k in range(n_half - 1):
        to = jnp.where(half <= k, k + 1, k)
        copy = pltpu.make_async_remote_copy(
            far.at[half], far.at[half], f_send.at[k], f_recv.at[half],
            device_id={"rows": (to * 2 + odd) * n_y + y, "cls": cls}, device_id_type=MESH,
        )
        copy.start()
        copies.append(copy)

    def one_hot(i, carry):
        at = pl.ds(pl.multiple_of(i * LANES, LANES), LANES)
        hot = onehot_t[:, at].T
        onehot[at, 0:LEAVES] = hot
        onehot[at, LEAVES : 2 * LEAVES] = hot
        return carry

    lax.fori_loop(0, blocks, one_hot, 0, unroll=8)

    for d in range(1, n_half):
        source = lax.rem(half + n_half - d, n_half)
        pltpu.make_async_remote_copy(
            far.at[source], far.at[source], f_send.at[d], f_recv.at[source],
            device_id=far_peer(d), device_id_type=MESH,
        ).wait_recv()
    total = far[0]
    for k in range(1, n_half):
        total = total + far[k]
    lv_t[mine] = -0.3 * total[0] / (total[1] + 1.0)

    for j in near_order:
        copy = pltpu.make_async_remote_copy(
            lv_t.at[mine], lv_t.at[mine], g_send.at[j], g_recv.at[j],
            device_id=near_peer(j), device_id_type=MESH,
        )
        copy.start()
        copies.append(copy)
    for j in range(1, 2 * n_y):
        dy, flip = j // 2, j % 2
        source = lax.rem(y + n_y - dy, n_y) * 2 + (1 - odd if flip else odd)
        pltpu.make_async_remote_copy(
            lv_t.at[source], lv_t.at[source], g_send.at[j], g_recv.at[j],
            device_id=near_peer(j), device_id_type=MESH,
        ).wait_recv()
    lv_out[...] = lv_t[...].reshape(width, LEAVES).T
    for copy in copies:
        copy.wait_send()


def update(x_v, onehot, lv, lv_hbm, up_hbm, up_v, sem):
    values = jnp.concatenate(split(lv[...]), axis=0)
    copies = [pltpu.make_async_copy(lv, lv_hbm, sem.at[WRITES])]
    copies[0].start()
    chunk_rows = x_v.shape[0] // WRITES
    for c in range(WRITES):
        def part(i, carry, c=c):
            at = pl.ds(pl.multiple_of(c * chunk_rows + i * 256, 256), 256)
            up_v[at, :] = x_v[at, :] + jnp.dot(onehot[at, :], values, preferred_element_type=F32)
            return carry

        lax.fori_loop(0, chunk_rows // 256, part, 0, unroll=2)
        at = pl.ds(c * chunk_rows, chunk_rows)
        copies.append(pltpu.make_async_copy(up_v.at[at], up_hbm.at[at], sem.at[c]))
        copies[-1].start()
    for copy in copies:
        copy.wait()


def solution(mesh):
    n_cls, n_rows = mesh.shape["cls"], mesh.shape["rows"]
    n_y = 4
    n_z = n_rows // n_y

    def per_device(logits, leaf_index, labels):
        rows, width = logits.shape
        blocks = rows // LANES
        piece = width // (2 * n_y)
        dma = pltpu.SemaphoreType.DMA
        vmem = pl.BlockSpec(memory_space=pltpu.VMEM)
        hbm = pl.BlockSpec(memory_space=pltpu.HBM)
        leaf_values, x_v, onehot = pl.pallas_call(
            functools.partial(kernel, n_cls, n_y, n_z),
            out_shape=(
                pltpu.VMEM((LEAVES, width), F32),
                pltpu.VMEM((rows, width), F32),
                pltpu.VMEM((rows, 2 * LEAVES), BF16),
            ),
            in_specs=[hbm, hbm, hbm],
            out_specs=(vmem, vmem, vmem),
            scratch_shapes=[
                pltpu.VMEM((blocks, LANES), jnp.int32),
                pltpu.VMEM((blocks, LANES), jnp.int32),
                pltpu.VMEM((width, rows), F32),
                pltpu.VMEM((2, PARTS, 2, blocks // PARTS, LANES), F32),
                pltpu.VMEM((n_cls // 2, PARTS, 2, blocks // PARTS, LANES), F32),
                pltpu.VMEM((LEAVES, rows), BF16),
                pltpu.VMEM((2, width, LEAVES), F32),
                pltpu.VMEM((2 * n_y, 2, piece, LEAVES), F32),
                pltpu.VMEM((n_z // 2, 2, piece, LEAVES), F32),
                pltpu.VMEM((2 * n_y, piece, LEAVES), F32),
                dma((CHUNKS + 2,)),
                dma((PARTS,)),
                dma((PARTS,)),
                dma((n_cls // 2, PARTS)),
                dma((n_cls // 2, PARTS)),
                dma((2 * n_y,)),
                dma((2 * n_y,)),
                dma((n_z // 2,)),
                dma((n_z // 2,)),
                dma((2 * n_y,)),
                dma((2 * n_y,)),
            ],
            compiler_params=pltpu.CompilerParams(
                collective_id=0, has_side_effects=True, vmem_limit_bytes=32 * 2**20
            ),
        )(
            in_hbm(logits),
            in_hbm(leaf_index.reshape(blocks, LANES)),
            in_hbm(labels.reshape(blocks, LANES)),
        )
        return pl.pallas_call(
            update,
            out_shape=(
                pltpu.HBM((LEAVES, width), F32),
                pltpu.HBM((rows, width), F32),
            ),
            in_specs=[vmem, vmem, vmem],
            out_specs=(hbm, hbm),
            scratch_shapes=[pltpu.VMEM((rows, width), F32), dma((WRITES + 1,))],
            compiler_params=pltpu.CompilerParams(vmem_limit_bytes=16 * 2**20),
        )(x_v, onehot, leaf_values)

    return jax.shard_map(
        per_device,
        mesh=mesh,
        in_specs=(P("rows", "cls"), P("rows"), P("rows")),
        out_specs=(P(None, "cls"), P("rows", "cls")),
        check_vma=False,
    )
```

```python
import functools

import jax
import jax.numpy as jnp
from jax import lax
from jax.experimental import pallas as pl
from jax.experimental.pallas import tpu as pltpu
from jax.sharding import PartitionSpec as P

LEAVES = 128
LANES = 128
MESH = pl.DeviceIdType.MESH
F32 = jnp.float32
BF16 = jnp.bfloat16
CHUNKS = 4
PARTS = 2
TOGETHER = 4
WRITES = 8


def in_hbm(array):
    return pltpu.with_memory_space_constraint(array, pltpu.HBM)


def split(value):
    high = value.astype(BF16)
    return high, (value - high.astype(F32)).astype(BF16)


def kernel(
    n_cls, n_y, n_z,
    x_hbm, leaf_hbm, label_hbm,
    lv_out, x_v, onehot,
    leaf_v, label_v, e_v, stats, chip, onehot_t, sums, near, far, lv_t,
    known, load_sem, c_send, c_recv, s_send, s_recv, r_send, r_recv, f_send, f_recv, g_send, g_recv,
):
    row, cls = lax.axis_index("rows"), lax.axis_index("cls")
    z, y = row // n_y, row % n_y
    half, odd = z // 2, z % 2
    n_half = n_z // 2
    rows, width = x_v.shape
    blocks = rows // LANES
    per_chunk = blocks // CHUNKS
    chunk_rows = rows // CHUNKS

    core = cls % 2
    n_x = n_cls // 2

    def core_peer():
        return {"rows": row, "cls": cls + 1 - 2 * core}

    def x_peer(d):
        return {"rows": row, "cls": lax.rem(cls + 2 * d, n_cls)}

    def near_place(j):
        dy, flip = j // 2, j % 2
        return lax.rem(y + dy, n_y), (1 - odd if flip else odd)

    def near_peer(j):
        to_y, to_odd = near_place(j)
        return {"rows": (half * 2 + to_odd) * n_y + to_y, "cls": cls}

    def z_peer(d):
        return {"rows": lax.rem(z + d + n_z, n_z) * n_y + y, "cls": cls}

    def far_peer(d):
        return {"rows": (lax.rem(half + d, n_half) * 2 + odd) * n_y + y, "cls": cls}

    loads = []
    for c in range(CHUNKS):
        part = pl.ds(c * chunk_rows, chunk_rows)
        loads.append(pltpu.make_async_copy(x_hbm.at[part], x_v.at[part], load_sem.at[c]))
    loads.append(pltpu.make_async_copy(leaf_hbm, leaf_v, load_sem.at[CHUNKS]))
    loads.append(pltpu.make_async_copy(label_hbm, label_v, load_sem.at[CHUNKS + 1]))
    for load in loads:
        load.start()

    barrier = pltpu.get_barrier_semaphore()
    near_order = sorted(range(1, 2 * n_y), key=lambda j: -(min(j // 2, n_y - j // 2) + j % 2))
    for j in near_order:
        pl.semaphore_signal(barrier, inc=1, device_id=near_peer(j), device_id_type=MESH)
    for d in range(1, n_x):
        pl.semaphore_signal(barrier, inc=1, device_id=x_peer(d), device_id_type=MESH)
    pl.semaphore_signal(barrier, inc=1, device_id=core_peer(), device_id_type=MESH)
    pl.semaphore_signal(barrier, inc=1, device_id=z_peer(2 * odd - 1), device_id_type=MESH)

    def tell(step):
        for side in range(2):
            pl.semaphore_signal(
                known.at[step, side], inc=1,
                device_id=z_peer((1 - 2 * side) * 2**step), device_id_type=MESH,
            )

    def hear(step):
        for side in range(2):
            pl.semaphore_wait(known.at[step, side], 1)

    per_part = blocks // PARTS
    for c in range(CHUNKS):
        loads[c].wait()

        def local(i, carry, c=c):
            k = c * per_chunk + i
            at = pl.ds(pl.multiple_of(k * LANES, LANES), LANES)
            xt = x_v[at, :].T
            peak = jnp.max(xt, axis=0, keepdims=True)
            expo = jnp.exp(xt - peak)
            e_v[:, at] = expo
            h = c * per_chunk // per_part
            at = pl.ds(k - h * per_part, 1)
            stats[0, h, 0, at, :] = peak
            stats[0, h, 1, at, :] = jnp.sum(expo, axis=0, keepdims=True)
            return carry

        lax.fori_loop(0, per_chunk, local, 0, unroll=8)

    pl.semaphore_wait(barrier, n_x + 2 * n_y)
    swaps = []
    for h in range(PARTS):
        copy = pltpu.make_async_remote_copy(
            stats.at[0, h], stats.at[1, h], c_send.at[h], c_recv.at[h],
            device_id=core_peer(), device_id_type=MESH,
        )
        copy.start()
        swaps.append(copy)
    tell(0)
    exchanges = []
    for h in range(PARTS):
        swaps[h].wait()
        peak = jnp.maximum(stats[0, h, 0], stats[1, h, 0])
        chip[0, h, 0] = peak
        chip[0, h, 1] = (
            stats[0, h, 1] * jnp.exp(stats[0, h, 0] - peak)
            + stats[1, h, 1] * jnp.exp(stats[1, h, 0] - peak)
        )
        for d in range(1, n_x):
            copy = pltpu.make_async_remote_copy(
                chip.at[0, h], chip.at[d, h], s_send.at[d, h], s_recv.at[d, h],
                device_id=x_peer(d), device_id_type=MESH,
            )
            copy.start()
            exchanges.append(copy)

    loads[CHUNKS].wait()
    loads[CHUNKS + 1].wait()

    def one_hot_t(i, carry):
        at = pl.ds(pl.multiple_of(i * LANES, LANES), LANES)
        which = lax.broadcasted_iota(jnp.int32, (LEAVES, LANES), 0)
        onehot_t[:, at] = (which == leaf_v[pl.ds(i, 1), :]).astype(F32).astype(BF16)
        return carry

    lax.fori_loop(0, blocks, one_hot_t, 0, unroll=4)

    hear(0)
    tell(1)
    piece = width // (2 * n_y)

    classes = lax.broadcasted_iota(jnp.int32, (width, LANES), 0) + cls * width
    acc = None
    for h in range(PARTS):
        for d in range(1, n_x):
            exchanges[h * (n_x - 1) + d - 1].wait()
        peak = chip[0, h, 0]
        for d in range(1, n_x):
            peak = jnp.maximum(peak, chip[d, h, 0])
        total = chip[0, h, 1] * jnp.exp(chip[0, h, 0] - peak)
        for d in range(1, n_x):
            total = total + chip[d, h, 1] * jnp.exp(chip[d, h, 0] - peak)
        stats[0, h, 1] = jnp.exp(stats[0, h, 0] - peak) / total

        for k in range(h * per_part, (h + 1) * per_part, TOGETHER):
            grads, hessians = [], []
            for i in range(k, k + TOGETHER):
                at = slice(i * LANES, (i + 1) * LANES)
                inverse = i - h * per_part
                prob = e_v[:, at] * stats[0, h, 1, inverse : inverse + 1, :]
                grads.append(prob - (classes == label_v[i : i + 1, :]).astype(F32))
                hessians.append(prob * (1.0 - prob))
            at = slice(k * LANES, (k + TOGETHER) * LANES)
            terms = split(jnp.concatenate(grads, axis=1)) + split(jnp.concatenate(hessians, axis=1))
            part = lax.dot_general(
                jnp.concatenate(terms, axis=0), onehot_t[:, at],
                (((1,), (1,)), ((), ())), preferred_element_type=F32,
            )
            acc = part if acc is None else acc + part
    sums[0] = acc[0:width] + acc[width : 2 * width]
    sums[1] = acc[2 * width : 3 * width] + acc[3 * width : 4 * width]

    shares = []
    for j in near_order:
        to_y, to_odd = near_place(j)
        theirs = pl.ds(pl.multiple_of((to_y * 2 + to_odd) * piece, piece), piece)
        copy = pltpu.make_async_remote_copy(
            sums.at[:, theirs], near.at[j], r_send.at[j], r_recv.at[j],
            device_id=near_peer(j), device_id_type=MESH,
        )
        copy.start()
        shares.append(copy)
    hear(1)
    tell(2)

    mine = y * 2 + odd
    own_part = pl.ds(pl.multiple_of(mine * piece, piece), piece)
    for copy in shares:
        copy.wait()
    total = sums[:, own_part, :]
    for j in range(1, 2 * n_y):
        total = total + near[j]
    far[half] = total

    hear(2)
    copies = []
    for k in range(n_half - 1):
        to = jnp.where(half <= k, k + 1, k)
        copy = pltpu.make_async_remote_copy(
            far.at[half], far.at[half], f_send.at[k], f_recv.at[half],
            device_id={"rows": (to * 2 + odd) * n_y + y, "cls": cls}, device_id_type=MESH,
        )
        copy.start()
        copies.append(copy)

    def one_hot(i, carry):
        at = pl.ds(pl.multiple_of(i * LANES, LANES), LANES)
        hot = onehot_t[:, at].T
        onehot[at, 0:LEAVES] = hot
        onehot[at, LEAVES : 2 * LEAVES] = hot
        return carry

    lax.fori_loop(0, blocks, one_hot, 0, unroll=8)

    for d in range(1, n_half):
        source = lax.rem(half + n_half - d, n_half)
        pltpu.make_async_remote_copy(
            far.at[source], far.at[source], f_send.at[d], f_recv.at[source],
            device_id=far_peer(d), device_id_type=MESH,
        ).wait_recv()
    total = far[0]
    for k in range(1, n_half):
        total = total + far[k]
    lv_t[mine] = -0.3 * total[0] / (total[1] + 1.0)

    for j in near_order:
        copy = pltpu.make_async_remote_copy(
            lv_t.at[mine], lv_t.at[mine], g_send.at[j], g_recv.at[j],
            device_id=near_peer(j), device_id_type=MESH,
        )
        copy.start()
        copies.append(copy)
    for j in range(1, 2 * n_y):
        dy, flip = j // 2, j % 2
        source = lax.rem(y + n_y - dy, n_y) * 2 + (1 - odd if flip else odd)
        pltpu.make_async_remote_copy(
            lv_t.at[source], lv_t.at[source], g_send.at[j], g_recv.at[j],
            device_id=near_peer(j), device_id_type=MESH,
        ).wait_recv()
    lv_out[...] = lv_t[...].reshape(width, LEAVES).T
    for copy in copies:
        copy.wait_send()


def update(x_v, onehot, lv, lv_hbm, up_hbm, up_v, sem):
    values = jnp.concatenate(split(lv[...]), axis=0)
    copies = [pltpu.make_async_copy(lv, lv_hbm, sem.at[WRITES])]
    copies[0].start()
    chunk_rows = x_v.shape[0] // WRITES
    for c in range(WRITES):
        def part(i, carry, c=c):
            at = pl.ds(pl.multiple_of(c * chunk_rows + i * 256, 256), 256)
            up_v[at, :] = x_v[at, :] + jnp.dot(onehot[at, :], values, preferred_element_type=F32)
            return carry

        lax.fori_loop(0, chunk_rows // 256, part, 0, unroll=2)
        at = pl.ds(c * chunk_rows, chunk_rows)
        copies.append(pltpu.make_async_copy(up_v.at[at], up_hbm.at[at], sem.at[c]))
        copies[-1].start()
    for copy in copies:
        copy.wait()


def solution(mesh):
    n_cls, n_rows = mesh.shape["cls"], mesh.shape["rows"]
    n_y = 4
    n_z = n_rows // n_y
    assert n_z == 16

    def per_device(logits, leaf_index, labels):
        rows, width = logits.shape
        blocks = rows // LANES
        piece = width // (2 * n_y)
        dma = pltpu.SemaphoreType.DMA
        vmem = pl.BlockSpec(memory_space=pltpu.VMEM)
        hbm = pl.BlockSpec(memory_space=pltpu.HBM)
        leaf_values, x_v, onehot = pl.pallas_call(
            functools.partial(kernel, n_cls, n_y, n_z),
            out_shape=(
                pltpu.VMEM((LEAVES, width), F32),
                pltpu.VMEM((rows, width), F32),
                pltpu.VMEM((rows, 2 * LEAVES), BF16),
            ),
            in_specs=[hbm, hbm, hbm],
            out_specs=(vmem, vmem, vmem),
            scratch_shapes=[
                pltpu.VMEM((blocks, LANES), jnp.int32),
                pltpu.VMEM((blocks, LANES), jnp.int32),
                pltpu.VMEM((width, rows), F32),
                pltpu.VMEM((2, PARTS, 2, blocks // PARTS, LANES), F32),
                pltpu.VMEM((n_cls // 2, PARTS, 2, blocks // PARTS, LANES), F32),
                pltpu.VMEM((LEAVES, rows), BF16),
                pltpu.VMEM((2, width, LEAVES), F32),
                pltpu.VMEM((2 * n_y, 2, piece, LEAVES), F32),
                pltpu.VMEM((n_z // 2, 2, piece, LEAVES), F32),
                pltpu.VMEM((2 * n_y, piece, LEAVES), F32),
                pltpu.SemaphoreType.REGULAR((3, 2)),
                dma((CHUNKS + 2,)),
                dma((PARTS,)),
                dma((PARTS,)),
                dma((n_cls // 2, PARTS)),
                dma((n_cls // 2, PARTS)),
                dma((2 * n_y,)),
                dma((2 * n_y,)),
                dma((n_z // 2,)),
                dma((n_z // 2,)),
                dma((2 * n_y,)),
                dma((2 * n_y,)),
            ],
            compiler_params=pltpu.CompilerParams(
                collective_id=0, has_side_effects=True, vmem_limit_bytes=32 * 2**20
            ),
        )(
            in_hbm(logits),
            in_hbm(leaf_index.reshape(blocks, LANES)),
            in_hbm(labels.reshape(blocks, LANES)),
        )
        return pl.pallas_call(
            update,
            out_shape=(
                pltpu.HBM((LEAVES, width), F32),
                pltpu.HBM((rows, width), F32),
            ),
            in_specs=[vmem, vmem, vmem],
            out_specs=(hbm, hbm),
            scratch_shapes=[pltpu.VMEM((rows, width), F32), dma((WRITES + 1,))],
            compiler_params=pltpu.CompilerParams(vmem_limit_bytes=16 * 2**20),
        )(x_v, onehot, leaf_values)

    return jax.shard_map(
        per_device,
        mesh=mesh,
        in_specs=(P("rows", "cls"), P("rows"), P("rows")),
        out_specs=(P(None, "cls"), P("rows", "cls")),
        check_vma=False,
    )
```

```python
import functools

import jax
import jax.numpy as jnp
from jax import lax
from jax.experimental import pallas as pl
from jax.experimental.pallas import tpu as pltpu
from jax.sharding import PartitionSpec as P

LEAVES = 128
LANES = 128
MESH = pl.DeviceIdType.MESH
F32 = jnp.float32
BF16 = jnp.bfloat16
CHUNKS = 4
PARTS = 2
TOGETHER = 4
WRITES = 8


def in_hbm(array):
    return pltpu.with_memory_space_constraint(array, pltpu.HBM)


def split(value):
    high = value.astype(BF16)
    return high, (value - high.astype(F32)).astype(BF16)


def kernel(
    n_cls, n_y, n_z,
    x_hbm, leaf_hbm, label_hbm,
    lv_out, x_v, onehot,
    leaf_v, label_v, e_v, stats, chip, onehot_t, sums, near, far, lv_t,
    known, load_sem, c_send, c_recv, s_send, s_recv, r_send, r_recv, f_send, f_recv, g_send, g_recv,
):
    row, cls = lax.axis_index("rows"), lax.axis_index("cls")
    z, y = row // n_y, row % n_y
    half, odd = z // 2, z % 2
    n_half = n_z // 2

    def role_of(of_half, of_odd):
        return lax.rem(of_odd + of_half // (n_half // 2), 2)

    role = role_of(half, odd)
    rows, width = x_v.shape
    blocks = rows // LANES
    per_chunk = blocks // CHUNKS
    chunk_rows = rows // CHUNKS

    core = cls % 2
    n_x = n_cls // 2

    def core_peer():
        return {"rows": row, "cls": cls + 1 - 2 * core}

    def x_peer(d):
        return {"rows": row, "cls": lax.rem(cls + 2 * d, n_cls)}

    def near_place(j):
        dy, flip = j // 2, j % 2
        return lax.rem(y + dy, n_y), (1 - role if flip else role)

    def near_peer(j):
        dy, flip = j // 2, j % 2
        to_odd = 1 - odd if flip else odd
        return {"rows": (half * 2 + to_odd) * n_y + lax.rem(y + dy, n_y), "cls": cls}

    def z_peer(d):
        return {"rows": lax.rem(z + d + n_z, n_z) * n_y + y, "cls": cls}

    def far_peer(to):
        return {"rows": (to * 2 + role_of(to, role)) * n_y + y, "cls": cls}

    loads = []
    for c in range(CHUNKS):
        part = pl.ds(c * chunk_rows, chunk_rows)
        loads.append(pltpu.make_async_copy(x_hbm.at[part], x_v.at[part], load_sem.at[c]))
    loads.append(pltpu.make_async_copy(leaf_hbm, leaf_v, load_sem.at[CHUNKS]))
    loads.append(pltpu.make_async_copy(label_hbm, label_v, load_sem.at[CHUNKS + 1]))
    for load in loads:
        load.start()

    barrier = pltpu.get_barrier_semaphore()
    near_order = sorted(range(1, 2 * n_y), key=lambda j: -(min(j // 2, n_y - j // 2) + j % 2))
    for j in near_order:
        pl.semaphore_signal(barrier, inc=1, device_id=near_peer(j), device_id_type=MESH)
    for d in range(1, n_x):
        pl.semaphore_signal(barrier, inc=1, device_id=x_peer(d), device_id_type=MESH)
    pl.semaphore_signal(barrier, inc=1, device_id=core_peer(), device_id_type=MESH)
    pl.semaphore_signal(barrier, inc=1, device_id=z_peer(2 * odd - 1), device_id_type=MESH)

    def tell(step):
        for side in range(2):
            pl.semaphore_signal(
                known.at[step, side], inc=1,
                device_id=z_peer((1 - 2 * side) * 2**step), device_id_type=MESH,
            )

    def hear(step):
        for side in range(2):
            pl.semaphore_wait(known.at[step, side], 1)

    per_part = blocks // PARTS
    for c in range(CHUNKS):
        loads[c].wait()

        def local(i, carry, c=c):
            k = c * per_chunk + i
            at = pl.ds(pl.multiple_of(k * LANES, LANES), LANES)
            xt = x_v[at, :].T
            peak = jnp.max(xt, axis=0, keepdims=True)
            expo = jnp.exp(xt - peak)
            e_v[:, at] = expo
            h = c * per_chunk // per_part
            at = pl.ds(k - h * per_part, 1)
            stats[0, h, 0, at, :] = peak
            stats[0, h, 1, at, :] = jnp.sum(expo, axis=0, keepdims=True)
            return carry

        lax.fori_loop(0, per_chunk, local, 0, unroll=8)

    pl.semaphore_wait(barrier, n_x + 2 * n_y)
    swaps = []
    for h in range(PARTS):
        copy = pltpu.make_async_remote_copy(
            stats.at[0, h], stats.at[1, h], c_send.at[h], c_recv.at[h],
            device_id=core_peer(), device_id_type=MESH,
        )
        copy.start()
        swaps.append(copy)
    tell(0)
    exchanges = []
    for h in range(PARTS):
        swaps[h].wait()
        peak = jnp.maximum(stats[0, h, 0], stats[1, h, 0])
        chip[0, h, 0] = peak
        chip[0, h, 1] = (
            stats[0, h, 1] * jnp.exp(stats[0, h, 0] - peak)
            + stats[1, h, 1] * jnp.exp(stats[1, h, 0] - peak)
        )
        for d in range(1, n_x):
            copy = pltpu.make_async_remote_copy(
                chip.at[0, h], chip.at[d, h], s_send.at[d, h], s_recv.at[d, h],
                device_id=x_peer(d), device_id_type=MESH,
            )
            copy.start()
            exchanges.append(copy)

    loads[CHUNKS].wait()
    loads[CHUNKS + 1].wait()

    def one_hot_t(i, carry):
        at = pl.ds(pl.multiple_of(i * LANES, LANES), LANES)
        which = lax.broadcasted_iota(jnp.int32, (LEAVES, LANES), 0)
        onehot_t[:, at] = (which == leaf_v[pl.ds(i, 1), :]).astype(F32).astype(BF16)
        return carry

    lax.fori_loop(0, blocks, one_hot_t, 0, unroll=4)

    hear(0)
    tell(1)
    piece = width // (2 * n_y)

    classes = lax.broadcasted_iota(jnp.int32, (width, LANES), 0) + cls * width
    acc = None
    for h in range(PARTS):
        for d in range(1, n_x):
            exchanges[h * (n_x - 1) + d - 1].wait()
        peak = chip[0, h, 0]
        for d in range(1, n_x):
            peak = jnp.maximum(peak, chip[d, h, 0])
        total = chip[0, h, 1] * jnp.exp(chip[0, h, 0] - peak)
        for d in range(1, n_x):
            total = total + chip[d, h, 1] * jnp.exp(chip[d, h, 0] - peak)
        stats[0, h, 1] = jnp.exp(stats[0, h, 0] - peak) / total

        for k in range(h * per_part, (h + 1) * per_part, TOGETHER):
            grads, hessians = [], []
            for i in range(k, k + TOGETHER):
                at = slice(i * LANES, (i + 1) * LANES)
                inverse = i - h * per_part
                prob = e_v[:, at] * stats[0, h, 1, inverse : inverse + 1, :]
                grads.append(prob - (classes == label_v[i : i + 1, :]).astype(F32))
                hessians.append(prob * (1.0 - prob))
            at = slice(k * LANES, (k + TOGETHER) * LANES)
            terms = split(jnp.concatenate(grads, axis=1)) + split(jnp.concatenate(hessians, axis=1))
            part = lax.dot_general(
                jnp.concatenate(terms, axis=0), onehot_t[:, at],
                (((1,), (1,)), ((), ())), preferred_element_type=F32,
            )
            acc = part if acc is None else acc + part
    sums[0] = acc[0:width] + acc[width : 2 * width]
    sums[1] = acc[2 * width : 3 * width] + acc[3 * width : 4 * width]

    shares = []
    for j in near_order:
        to_y, to_role = near_place(j)
        theirs = pl.ds(pl.multiple_of((to_y * 2 + to_role) * piece, piece), piece)
        copy = pltpu.make_async_remote_copy(
            sums.at[:, theirs], near.at[j], r_send.at[j], r_recv.at[j],
            device_id=near_peer(j), device_id_type=MESH,
        )
        copy.start()
        shares.append(copy)
    hear(1)
    tell(2)

    mine = y * 2 + role
    own_part = pl.ds(pl.multiple_of(mine * piece, piece), piece)
    for copy in shares:
        copy.wait()
    total = sums[:, own_part, :]
    for j in range(1, 2 * n_y):
        total = total + near[j]
    far[half] = total

    hear(2)
    copies = []
    for k in range(n_half - 1):
        to = jnp.where(half <= k, k + 1, k)
        copy = pltpu.make_async_remote_copy(
            far.at[half], far.at[half], f_send.at[k], f_recv.at[half],
            device_id=far_peer(to), device_id_type=MESH,
        )
        copy.start()
        copies.append(copy)

    def one_hot(i, carry):
        at = pl.ds(pl.multiple_of(i * LANES, LANES), LANES)
        hot = onehot_t[:, at].T
        onehot[at, 0:LEAVES] = hot
        onehot[at, LEAVES : 2 * LEAVES] = hot
        return carry

    lax.fori_loop(0, blocks, one_hot, 0, unroll=8)

    for d in range(1, n_half):
        source = lax.rem(half + n_half - d, n_half)
        pltpu.make_async_remote_copy(
            far.at[source], far.at[source], f_send.at[d], f_recv.at[source],
            device_id=far_peer(source), device_id_type=MESH,
        ).wait_recv()
    total = far[0]
    for k in range(1, n_half):
        total = total + far[k]
    lv_t[mine] = -0.3 * total[0] / (total[1] + 1.0)

    for j in near_order:
        copy = pltpu.make_async_remote_copy(
            lv_t.at[mine], lv_t.at[mine], g_send.at[j], g_recv.at[j],
            device_id=near_peer(j), device_id_type=MESH,
        )
        copy.start()
        copies.append(copy)
    for j in range(1, 2 * n_y):
        dy, flip = j // 2, j % 2
        source = lax.rem(y + n_y - dy, n_y) * 2 + (1 - role if flip else role)
        pltpu.make_async_remote_copy(
            lv_t.at[source], lv_t.at[source], g_send.at[j], g_recv.at[j],
            device_id=near_peer(j), device_id_type=MESH,
        ).wait_recv()
    lv_out[...] = lv_t[...].reshape(width, LEAVES).T
    for copy in copies:
        copy.wait_send()


def update(x_v, onehot, lv, lv_hbm, up_hbm, up_v, sem):
    values = jnp.concatenate(split(lv[...]), axis=0)
    copies = [pltpu.make_async_copy(lv, lv_hbm, sem.at[WRITES])]
    copies[0].start()
    chunk_rows = x_v.shape[0] // WRITES
    for c in range(WRITES):
        def part(i, carry, c=c):
            at = pl.ds(pl.multiple_of(c * chunk_rows + i * 256, 256), 256)
            up_v[at, :] = x_v[at, :] + jnp.dot(onehot[at, :], values, preferred_element_type=F32)
            return carry

        lax.fori_loop(0, chunk_rows // 256, part, 0, unroll=2)
        at = pl.ds(c * chunk_rows, chunk_rows)
        copies.append(pltpu.make_async_copy(up_v.at[at], up_hbm.at[at], sem.at[c]))
        copies[-1].start()
    for copy in copies:
        copy.wait()


def solution(mesh):
    n_cls, n_rows = mesh.shape["cls"], mesh.shape["rows"]
    n_y = 4
    n_z = n_rows // n_y
    assert n_z == 16

    def per_device(logits, leaf_index, labels):
        rows, width = logits.shape
        blocks = rows // LANES
        piece = width // (2 * n_y)
        dma = pltpu.SemaphoreType.DMA
        vmem = pl.BlockSpec(memory_space=pltpu.VMEM)
        hbm = pl.BlockSpec(memory_space=pltpu.HBM)
        leaf_values, x_v, onehot = pl.pallas_call(
            functools.partial(kernel, n_cls, n_y, n_z),
            out_shape=(
                pltpu.VMEM((LEAVES, width), F32),
                pltpu.VMEM((rows, width), F32),
                pltpu.VMEM((rows, 2 * LEAVES), BF16),
            ),
            in_specs=[hbm, hbm, hbm],
            out_specs=(vmem, vmem, vmem),
            scratch_shapes=[
                pltpu.VMEM((blocks, LANES), jnp.int32),
                pltpu.VMEM((blocks, LANES), jnp.int32),
                pltpu.VMEM((width, rows), F32),
                pltpu.VMEM((2, PARTS, 2, blocks // PARTS, LANES), F32),
                pltpu.VMEM((n_cls // 2, PARTS, 2, blocks // PARTS, LANES), F32),
                pltpu.VMEM((LEAVES, rows), BF16),
                pltpu.VMEM((2, width, LEAVES), F32),
                pltpu.VMEM((2 * n_y, 2, piece, LEAVES), F32),
                pltpu.VMEM((n_z // 2, 2, piece, LEAVES), F32),
                pltpu.VMEM((2 * n_y, piece, LEAVES), F32),
                pltpu.SemaphoreType.REGULAR((3, 2)),
                dma((CHUNKS + 2,)),
                dma((PARTS,)),
                dma((PARTS,)),
                dma((n_cls // 2, PARTS)),
                dma((n_cls // 2, PARTS)),
                dma((2 * n_y,)),
                dma((2 * n_y,)),
                dma((n_z // 2,)),
                dma((n_z // 2,)),
                dma((2 * n_y,)),
                dma((2 * n_y,)),
            ],
            compiler_params=pltpu.CompilerParams(
                collective_id=0, has_side_effects=True, vmem_limit_bytes=32 * 2**20
            ),
        )(
            in_hbm(logits),
            in_hbm(leaf_index.reshape(blocks, LANES)),
            in_hbm(labels.reshape(blocks, LANES)),
        )
        return pl.pallas_call(
            update,
            out_shape=(
                pltpu.HBM((LEAVES, width), F32),
                pltpu.HBM((rows, width), F32),
            ),
            in_specs=[vmem, vmem, vmem],
            out_specs=(hbm, hbm),
            scratch_shapes=[pltpu.VMEM((rows, width), F32), dma((WRITES + 1,))],
            compiler_params=pltpu.CompilerParams(vmem_limit_bytes=16 * 2**20),
        )(x_v, onehot, leaf_values)

    return jax.shard_map(
        per_device,
        mesh=mesh,
        in_specs=(P("rows", "cls"), P("rows"), P("rows")),
        out_specs=(P(None, "cls"), P("rows", "cls")),
        check_vma=False,
    )
```

```python
import functools

import jax
import jax.numpy as jnp
from jax import lax
from jax.experimental import pallas as pl
from jax.experimental.pallas import tpu as pltpu
from jax.sharding import PartitionSpec as P

LEAVES = 128
LANES = 128
MESH = pl.DeviceIdType.MESH
F32 = jnp.float32
BF16 = jnp.bfloat16
CHUNKS = 4
PARTS = 2
TOGETHER = 4
WRITES = 8


def in_hbm(array):
    return pltpu.with_memory_space_constraint(array, pltpu.HBM)


def split(value):
    high = value.astype(BF16)
    return high, (value - high.astype(F32)).astype(BF16)


def kernel(
    n_cls, n_y, n_z,
    x_hbm, leaf_hbm, label_hbm,
    lv_out, x_v, onehot,
    leaf_v, label_v, e_v, stats, chip, onehot_t, sums, near, far, other, lv_t,
    known, load_sem, c_send, c_recv, s_send, s_recv, r_send, r_recv, f_send, f_recv, o_send, o_recv, g_send, g_recv,
):
    row, cls = lax.axis_index("rows"), lax.axis_index("cls")
    z, y = row // n_y, row % n_y
    half, odd = z // 2, z % 2
    n_half = n_z // 2

    def role_of(of_half, of_odd):
        return jnp.where(of_half == n_half // 2, 1 - of_odd, of_odd)

    role = role_of(half, odd)
    rows, width = x_v.shape
    blocks = rows // LANES
    per_chunk = blocks // CHUNKS
    chunk_rows = rows // CHUNKS

    core = cls % 2
    n_x = n_cls // 2

    def core_peer():
        return {"rows": row, "cls": cls + 1 - 2 * core}

    def x_peer(d):
        return {"rows": row, "cls": lax.rem(cls + 2 * d, n_cls)}

    def near_place(j):
        dy, flip = j // 2, j % 2
        return lax.rem(y + dy, n_y), (1 - role if flip else role)

    def near_peer(j):
        dy, flip = j // 2, j % 2
        to_odd = 1 - odd if flip else odd
        return {"rows": (half * 2 + to_odd) * n_y + lax.rem(y + dy, n_y), "cls": cls}

    def z_peer(d):
        return {"rows": lax.rem(z + d + n_z, n_z) * n_y + y, "cls": cls}

    def far_peer(to):
        return {"rows": (to * 2 + role_of(to, role)) * n_y + y, "cls": cls}

    loads = []
    for c in range(CHUNKS):
        part = pl.ds(c * chunk_rows, chunk_rows)
        loads.append(pltpu.make_async_copy(x_hbm.at[part], x_v.at[part], load_sem.at[c]))
    loads.append(pltpu.make_async_copy(leaf_hbm, leaf_v, load_sem.at[CHUNKS]))
    loads.append(pltpu.make_async_copy(label_hbm, label_v, load_sem.at[CHUNKS + 1]))
    for load in loads:
        load.start()

    barrier = pltpu.get_barrier_semaphore()
    near_order = sorted(range(1, 2 * n_y), key=lambda j: -(min(j // 2, n_y - j // 2) + j % 2))
    for j in near_order:
        pl.semaphore_signal(barrier, inc=1, device_id=near_peer(j), device_id_type=MESH)
    for d in range(1, n_x):
        pl.semaphore_signal(barrier, inc=1, device_id=x_peer(d), device_id_type=MESH)
    pl.semaphore_signal(barrier, inc=1, device_id=core_peer(), device_id_type=MESH)
    pl.semaphore_signal(barrier, inc=1, device_id=z_peer(2 * odd - 1), device_id_type=MESH)

    def tell(step):
        for side in range(2):
            pl.semaphore_signal(
                known.at[step, side], inc=1,
                device_id=z_peer((1 - 2 * side) * 2**step), device_id_type=MESH,
            )

    def hear(step):
        for side in range(2):
            pl.semaphore_wait(known.at[step, side], 1)

    per_part = blocks // PARTS
    for c in range(CHUNKS):
        loads[c].wait()

        def local(i, carry, c=c):
            k = c * per_chunk + i
            at = pl.ds(pl.multiple_of(k * LANES, LANES), LANES)
            xt = x_v[at, :].T
            peak = jnp.max(xt, axis=0, keepdims=True)
            expo = jnp.exp(xt - peak)
            e_v[:, at] = expo
            h = c * per_chunk // per_part
            at = pl.ds(k - h * per_part, 1)
            stats[0, h, 0, at, :] = peak
            stats[0, h, 1, at, :] = jnp.sum(expo, axis=0, keepdims=True)
            return carry

        lax.fori_loop(0, per_chunk, local, 0, unroll=8)

    pl.semaphore_wait(barrier, n_x + 2 * n_y)
    swaps = []
    for h in range(PARTS):
        copy = pltpu.make_async_remote_copy(
            stats.at[0, h], stats.at[1, h], c_send.at[h], c_recv.at[h],
            device_id=core_peer(), device_id_type=MESH,
        )
        copy.start()
        swaps.append(copy)
    tell(0)
    exchanges = []
    for h in range(PARTS):
        swaps[h].wait()
        peak = jnp.maximum(stats[0, h, 0], stats[1, h, 0])
        chip[0, h, 0] = peak
        chip[0, h, 1] = (
            stats[0, h, 1] * jnp.exp(stats[0, h, 0] - peak)
            + stats[1, h, 1] * jnp.exp(stats[1, h, 0] - peak)
        )
        for d in range(1, n_x):
            copy = pltpu.make_async_remote_copy(
                chip.at[0, h], chip.at[d, h], s_send.at[d, h], s_recv.at[d, h],
                device_id=x_peer(d), device_id_type=MESH,
            )
            copy.start()
            exchanges.append(copy)

    loads[CHUNKS].wait()
    loads[CHUNKS + 1].wait()

    def one_hot_t(i, carry):
        at = pl.ds(pl.multiple_of(i * LANES, LANES), LANES)
        which = lax.broadcasted_iota(jnp.int32, (LEAVES, LANES), 0)
        onehot_t[:, at] = (which == leaf_v[pl.ds(i, 1), :]).astype(F32).astype(BF16)
        return carry

    lax.fori_loop(0, blocks, one_hot_t, 0, unroll=4)

    hear(0)
    tell(1)
    piece = width // (2 * n_y)

    classes = lax.broadcasted_iota(jnp.int32, (width, LANES), 0) + cls * width
    acc = None
    for h in range(PARTS):
        for d in range(1, n_x):
            exchanges[h * (n_x - 1) + d - 1].wait()
        peak = chip[0, h, 0]
        for d in range(1, n_x):
            peak = jnp.maximum(peak, chip[d, h, 0])
        total = chip[0, h, 1] * jnp.exp(chip[0, h, 0] - peak)
        for d in range(1, n_x):
            total = total + chip[d, h, 1] * jnp.exp(chip[d, h, 0] - peak)
        stats[0, h, 1] = jnp.exp(stats[0, h, 0] - peak) / total

        for k in range(h * per_part, (h + 1) * per_part, TOGETHER):
            grads, hessians = [], []
            for i in range(k, k + TOGETHER):
                at = slice(i * LANES, (i + 1) * LANES)
                inverse = i - h * per_part
                prob = e_v[:, at] * stats[0, h, 1, inverse : inverse + 1, :]
                grads.append(prob - (classes == label_v[i : i + 1, :]).astype(F32))
                hessians.append(prob * (1.0 - prob))
            at = slice(k * LANES, (k + TOGETHER) * LANES)
            terms = split(jnp.concatenate(grads, axis=1)) + split(jnp.concatenate(hessians, axis=1))
            part = lax.dot_general(
                jnp.concatenate(terms, axis=0), onehot_t[:, at],
                (((1,), (1,)), ((), ())), preferred_element_type=F32,
            )
            acc = part if acc is None else acc + part
    sums[0] = acc[0:width] + acc[width : 2 * width]
    sums[1] = acc[2 * width : 3 * width] + acc[3 * width : 4 * width]

    shares = []
    for j in near_order:
        to_y, to_role = near_place(j)
        theirs = pl.ds(pl.multiple_of((to_y * 2 + to_role) * piece, piece), piece)
        copy = pltpu.make_async_remote_copy(
            sums.at[:, theirs], near.at[j], r_send.at[j], r_recv.at[j],
            device_id=near_peer(j), device_id_type=MESH,
        )
        copy.start()
        shares.append(copy)
    hear(1)
    tell(2)

    mine = y * 2 + role
    own_part = pl.ds(pl.multiple_of(mine * piece, piece), piece)
    for copy in shares:
        copy.wait()
    total = sums[:, own_part, :]
    for j in range(1, 2 * n_y):
        total = total + near[j]
    far[half] = total

    hear(2)
    copies = []
    for k in range(n_half - 1):
        to = jnp.where(half <= k, k + 1, k)
        copy = pltpu.make_async_remote_copy(
            far.at[half], far.at[half], f_send.at[k], f_recv.at[half],
            device_id=far_peer(to), device_id_type=MESH,
        )
        copy.start()
        copies.append(copy)
        if k == 0:
            copy = pltpu.make_async_remote_copy(
                far.at[half], other.at[half], o_send.at[0], o_recv.at[half],
                device_id={"rows": (1 - role) * n_y + y, "cls": cls}, device_id_type=MESH,
            )
            copy.start()
            copies.append(copy)

    def one_hot(i, carry):
        at = pl.ds(pl.multiple_of(i * LANES, LANES), LANES)
        hot = onehot_t[:, at].T
        onehot[at, 0:LEAVES] = hot
        onehot[at, LEAVES : 2 * LEAVES] = hot
        return carry

    lax.fori_loop(0, blocks, one_hot, 0, unroll=8)

    for d in range(1, n_half):
        source = lax.rem(half + n_half - d, n_half)
        pltpu.make_async_remote_copy(
            far.at[source], far.at[source], f_send.at[d], f_recv.at[source],
            device_id=far_peer(source), device_id_type=MESH,
        ).wait_recv()
    def values(parts):
        total = parts[0]
        for k in range(1, n_half):
            total = total + parts[k]
        return -0.3 * total[0] / (total[1] + 1.0)

    lv_t[mine] = values(far)

    @pl.when(half == 0)
    def _():
        for k in range(n_half):
            pltpu.make_async_remote_copy(
                other.at[k], other.at[k], o_send.at[0], o_recv.at[k],
                device_id=core_peer(), device_id_type=MESH,
            ).wait_recv()
        lv_t[y * 2 + 1 - role] = values(other)
        gathers = []
        for dy in (2, 1, 3):
            both = lv_t.at[pl.ds(y * 2, 2)]
            copy = pltpu.make_async_remote_copy(
                both, both, g_send.at[2 * dy], g_recv.at[2 * dy],
                device_id=near_peer(2 * dy), device_id_type=MESH,
            )
            copy.start()
            gathers.append(copy)
        for dy in (1, 3, 2):
            both = lv_t.at[pl.ds(lax.rem(y + n_y - dy, n_y) * 2, 2)]
            pltpu.make_async_remote_copy(
                both, both, g_send.at[2 * dy], g_recv.at[2 * dy],
                device_id=near_peer(2 * dy), device_id_type=MESH,
            ).wait_recv()
        for copy in gathers:
            copy.wait_send()

    @pl.when(half != 0)
    def _():
        gathers = []
        for j in near_order:
            copy = pltpu.make_async_remote_copy(
                lv_t.at[mine], lv_t.at[mine], g_send.at[j], g_recv.at[j],
                device_id=near_peer(j), device_id_type=MESH,
            )
            copy.start()
            gathers.append(copy)
        for j in range(1, 2 * n_y):
            dy, flip = j // 2, j % 2
            source = lax.rem(y + n_y - dy, n_y) * 2 + (1 - role if flip else role)
            pltpu.make_async_remote_copy(
                lv_t.at[source], lv_t.at[source], g_send.at[j], g_recv.at[j],
                device_id=near_peer(j), device_id_type=MESH,
            ).wait_recv()
        for copy in gathers:
            copy.wait_send()

    lv_out[...] = lv_t[...].reshape(width, LEAVES).T
    for copy in copies:
        copy.wait_send()


def update(x_v, onehot, lv, lv_hbm, up_hbm, up_v, sem):
    values = jnp.concatenate(split(lv[...]), axis=0)
    copies = [pltpu.make_async_copy(lv, lv_hbm, sem.at[WRITES])]
    copies[0].start()
    chunk_rows = x_v.shape[0] // WRITES
    for c in range(WRITES):
        def part(i, carry, c=c):
            at = pl.ds(pl.multiple_of(c * chunk_rows + i * 256, 256), 256)
            up_v[at, :] = x_v[at, :] + jnp.dot(onehot[at, :], values, preferred_element_type=F32)
            return carry

        lax.fori_loop(0, chunk_rows // 256, part, 0, unroll=2)
        at = pl.ds(c * chunk_rows, chunk_rows)
        copies.append(pltpu.make_async_copy(up_v.at[at], up_hbm.at[at], sem.at[c]))
        copies[-1].start()
    for copy in copies:
        copy.wait()


def solution(mesh):
    n_cls, n_rows = mesh.shape["cls"], mesh.shape["rows"]
    n_y = 4
    n_z = n_rows // n_y
    assert n_z == 16

    def per_device(logits, leaf_index, labels):
        rows, width = logits.shape
        blocks = rows // LANES
        piece = width // (2 * n_y)
        dma = pltpu.SemaphoreType.DMA
        vmem = pl.BlockSpec(memory_space=pltpu.VMEM)
        hbm = pl.BlockSpec(memory_space=pltpu.HBM)
        leaf_values, x_v, onehot = pl.pallas_call(
            functools.partial(kernel, n_cls, n_y, n_z),
            out_shape=(
                pltpu.VMEM((LEAVES, width), F32),
                pltpu.VMEM((rows, width), F32),
                pltpu.VMEM((rows, 2 * LEAVES), BF16),
            ),
            in_specs=[hbm, hbm, hbm],
            out_specs=(vmem, vmem, vmem),
            scratch_shapes=[
                pltpu.VMEM((blocks, LANES), jnp.int32),
                pltpu.VMEM((blocks, LANES), jnp.int32),
                pltpu.VMEM((width, rows), F32),
                pltpu.VMEM((2, PARTS, 2, blocks // PARTS, LANES), F32),
                pltpu.VMEM((n_cls // 2, PARTS, 2, blocks // PARTS, LANES), F32),
                pltpu.VMEM((LEAVES, rows), BF16),
                pltpu.VMEM((2, width, LEAVES), F32),
                pltpu.VMEM((2 * n_y, 2, piece, LEAVES), F32),
                pltpu.VMEM((n_z // 2, 2, piece, LEAVES), F32),
                pltpu.VMEM((n_z // 2, 2, piece, LEAVES), F32),
                pltpu.VMEM((2 * n_y, piece, LEAVES), F32),
                pltpu.SemaphoreType.REGULAR((3, 2)),
                dma((CHUNKS + 2,)),
                dma((PARTS,)),
                dma((PARTS,)),
                dma((n_cls // 2, PARTS)),
                dma((n_cls // 2, PARTS)),
                dma((2 * n_y,)),
                dma((2 * n_y,)),
                dma((n_z // 2,)),
                dma((n_z // 2,)),
                dma((1,)),
                dma((n_z // 2,)),
                dma((2 * n_y,)),
                dma((2 * n_y,)),
            ],
            compiler_params=pltpu.CompilerParams(
                collective_id=0, has_side_effects=True, vmem_limit_bytes=32 * 2**20
            ),
        )(
            in_hbm(logits),
            in_hbm(leaf_index.reshape(blocks, LANES)),
            in_hbm(labels.reshape(blocks, LANES)),
        )
        return pl.pallas_call(
            update,
            out_shape=(
                pltpu.HBM((LEAVES, width), F32),
                pltpu.HBM((rows, width), F32),
            ),
            in_specs=[vmem, vmem, vmem],
            out_specs=(hbm, hbm),
            scratch_shapes=[pltpu.VMEM((rows, width), F32), dma((WRITES + 1,))],
            compiler_params=pltpu.CompilerParams(vmem_limit_bytes=16 * 2**20),
        )(x_v, onehot, leaf_values)

    return jax.shard_map(
        per_device,
        mesh=mesh,
        in_specs=(P("rows", "cls"), P("rows"), P("rows")),
        out_specs=(P(None, "cls"), P("rows", "cls")),
        check_vma=False,
    )
```

```python
import functools

import jax
import jax.numpy as jnp
from jax import lax
from jax.experimental import pallas as pl
from jax.experimental.pallas import tpu as pltpu
from jax.sharding import PartitionSpec as P

LEAVES = 128
LANES = 128
MESH = pl.DeviceIdType.MESH
F32 = jnp.float32
BF16 = jnp.bfloat16
CHUNKS = 4
PARTS = 2
TOGETHER = 4
WRITES = 8


def in_hbm(array):
    return pltpu.with_memory_space_constraint(array, pltpu.HBM)


def split(value):
    high = value.astype(BF16)
    return high, (value - high.astype(F32)).astype(BF16)


def kernel(
    n_cls, n_y, n_z,
    x_hbm, leaf_hbm, label_hbm,
    lv_out, x_v, onehot,
    leaf_v, label_v, e_v, stats, chip, onehot_t, sums, near, far, lv_t,
    known, load_sem, c_send, c_recv, s_send, s_recv, r_send, r_recv, f_send, f_recv, g_send, g_recv,
):
    row, cls = lax.axis_index("rows"), lax.axis_index("cls")
    z, y = row // n_y, row % n_y
    half, odd = z // 2, z % 2
    n_half = n_z // 2

    def role_of(of_half, of_odd):
        return jnp.where(of_half == n_half // 2, 1 - of_odd, of_odd)

    role = role_of(half, odd)
    rows, width = x_v.shape
    blocks = rows // LANES
    per_chunk = blocks // CHUNKS
    chunk_rows = rows // CHUNKS

    core = cls % 2
    n_x = n_cls // 2

    def core_peer():
        return {"rows": row, "cls": cls + 1 - 2 * core}

    def x_peer(d):
        return {"rows": row, "cls": lax.rem(cls + 2 * d, n_cls)}

    def near_place(j):
        dy, flip = j // 2, j % 2
        return lax.rem(y + dy, n_y), (1 - role if flip else role)

    def near_peer(j):
        dy, flip = j // 2, j % 2
        to_odd = 1 - odd if flip else odd
        return {"rows": (half * 2 + to_odd) * n_y + lax.rem(y + dy, n_y), "cls": cls}

    def z_peer(d):
        return {"rows": lax.rem(z + d + n_z, n_z) * n_y + y, "cls": cls}

    def far_peer(to):
        return {"rows": (to * 2 + role_of(to, role)) * n_y + y, "cls": cls}

    loads = []
    for c in range(CHUNKS):
        part = pl.ds(c * chunk_rows, chunk_rows)
        loads.append(pltpu.make_async_copy(x_hbm.at[part], x_v.at[part], load_sem.at[c]))
    loads.append(pltpu.make_async_copy(leaf_hbm, leaf_v, load_sem.at[CHUNKS]))
    loads.append(pltpu.make_async_copy(label_hbm, label_v, load_sem.at[CHUNKS + 1]))
    for load in loads:
        load.start()

    barrier = pltpu.get_barrier_semaphore()
    near_order = sorted(range(1, 2 * n_y), key=lambda j: -(min(j // 2, n_y - j // 2) + j % 2))
    for j in near_order:
        pl.semaphore_signal(barrier, inc=1, device_id=near_peer(j), device_id_type=MESH)
    for d in range(1, n_x):
        pl.semaphore_signal(barrier, inc=1, device_id=x_peer(d), device_id_type=MESH)
    pl.semaphore_signal(barrier, inc=1, device_id=core_peer(), device_id_type=MESH)
    pl.semaphore_signal(barrier, inc=1, device_id=z_peer(2 * odd - 1), device_id_type=MESH)

    def tell(step):
        for side in range(2):
            pl.semaphore_signal(
                known.at[step, side], inc=1,
                device_id=z_peer((1 - 2 * side) * 2**step), device_id_type=MESH,
            )

    def hear(step):
        for side in range(2):
            pl.semaphore_wait(known.at[step, side], 1)

    per_part = blocks // PARTS
    for c in range(CHUNKS):
        loads[c].wait()

        def local(i, carry, c=c):
            k = c * per_chunk + i
            at = pl.ds(pl.multiple_of(k * LANES, LANES), LANES)
            xt = x_v[at, :].T
            peak = jnp.max(xt, axis=0, keepdims=True)
            expo = jnp.exp(xt - peak)
            e_v[:, at] = expo
            h = c * per_chunk // per_part
            at = pl.ds(k - h * per_part, 1)
            stats[0, h, 0, at, :] = peak
            stats[0, h, 1, at, :] = jnp.sum(expo, axis=0, keepdims=True)
            return carry

        lax.fori_loop(0, per_chunk, local, 0, unroll=8)

    pl.semaphore_wait(barrier, n_x + 2 * n_y)
    swaps = []
    for h in range(PARTS):
        copy = pltpu.make_async_remote_copy(
            stats.at[0, h], stats.at[1, h], c_send.at[h], c_recv.at[h],
            device_id=core_peer(), device_id_type=MESH,
        )
        copy.start()
        swaps.append(copy)
    tell(0)
    exchanges = []
    for h in range(PARTS):
        swaps[h].wait()
        peak = jnp.maximum(stats[0, h, 0], stats[1, h, 0])
        chip[0, h, 0] = peak
        chip[0, h, 1] = (
            stats[0, h, 1] * jnp.exp(stats[0, h, 0] - peak)
            + stats[1, h, 1] * jnp.exp(stats[1, h, 0] - peak)
        )
        for d in range(1, n_x):
            copy = pltpu.make_async_remote_copy(
                chip.at[0, h], chip.at[d, h], s_send.at[d, h], s_recv.at[d, h],
                device_id=x_peer(d), device_id_type=MESH,
            )
            copy.start()
            exchanges.append(copy)

    loads[CHUNKS].wait()
    loads[CHUNKS + 1].wait()

    def one_hot_t(i, carry):
        at = pl.ds(pl.multiple_of(i * LANES, LANES), LANES)
        which = lax.broadcasted_iota(jnp.int32, (LEAVES, LANES), 0)
        onehot_t[:, at] = (which == leaf_v[pl.ds(i, 1), :]).astype(F32).astype(BF16)
        return carry

    lax.fori_loop(0, blocks, one_hot_t, 0, unroll=4)

    hear(0)
    tell(1)
    piece = width // (2 * n_y)

    classes = lax.broadcasted_iota(jnp.int32, (width, LANES), 0) + cls * width
    acc = None
    for h in range(PARTS):
        for d in range(1, n_x):
            exchanges[h * (n_x - 1) + d - 1].wait()
        peak = chip[0, h, 0]
        for d in range(1, n_x):
            peak = jnp.maximum(peak, chip[d, h, 0])
        total = chip[0, h, 1] * jnp.exp(chip[0, h, 0] - peak)
        for d in range(1, n_x):
            total = total + chip[d, h, 1] * jnp.exp(chip[d, h, 0] - peak)
        stats[0, h, 1] = jnp.exp(stats[0, h, 0] - peak) / total

        for k in range(h * per_part, (h + 1) * per_part, TOGETHER):
            grads, hessians = [], []
            for i in range(k, k + TOGETHER):
                at = slice(i * LANES, (i + 1) * LANES)
                inverse = i - h * per_part
                prob = e_v[:, at] * stats[0, h, 1, inverse : inverse + 1, :]
                grads.append(prob - (classes == label_v[i : i + 1, :]).astype(F32))
                hessians.append(prob * (1.0 - prob))
            at = slice(k * LANES, (k + TOGETHER) * LANES)
            terms = split(jnp.concatenate(grads, axis=1)) + split(jnp.concatenate(hessians, axis=1))
            part = lax.dot_general(
                jnp.concatenate(terms, axis=0), onehot_t[:, at],
                (((1,), (1,)), ((), ())), preferred_element_type=F32,
            )
            acc = part if acc is None else acc + part
    sums[0] = acc[0:width] + acc[width : 2 * width]
    sums[1] = acc[2 * width : 3 * width] + acc[3 * width : 4 * width]

    shares = []
    for j in near_order:
        to_y, to_role = near_place(j)
        theirs = pl.ds(pl.multiple_of((to_y * 2 + to_role) * piece, piece), piece)
        copy = pltpu.make_async_remote_copy(
            sums.at[:, theirs], near.at[j], r_send.at[j], r_recv.at[j],
            device_id=near_peer(j), device_id_type=MESH,
        )
        copy.start()
        shares.append(copy)
    hear(1)
    tell(2)

    mine = y * 2 + role
    own_part = pl.ds(pl.multiple_of(mine * piece, piece), piece)
    for copy in shares:
        copy.wait()
    total = sums[:, own_part, :]
    for j in range(1, 2 * n_y):
        total = total + near[j]
    far[half] = total

    hear(2)
    copies = []
    for k in range(n_half - 1):
        to = jnp.where(half <= k, k + 1, k)
        copy = pltpu.make_async_remote_copy(
            far.at[half], far.at[half], f_send.at[k], f_recv.at[half],
            device_id=far_peer(to), device_id_type=MESH,
        )
        copy.start()
        copies.append(copy)

    def one_hot(i, carry):
        at = pl.ds(pl.multiple_of(i * LANES, LANES), LANES)
        hot = onehot_t[:, at].T
        onehot[at, 0:LEAVES] = hot
        onehot[at, LEAVES : 2 * LEAVES] = hot
        return carry

    lax.fori_loop(0, blocks, one_hot, 0, unroll=8)

    for d in range(1, n_half):
        source = lax.rem(half + n_half - d, n_half)
        pltpu.make_async_remote_copy(
            far.at[source], far.at[source], f_send.at[d], f_recv.at[source],
            device_id=far_peer(source), device_id_type=MESH,
        ).wait_recv()
    total = far[0]
    for k in range(1, n_half):
        total = total + far[k]
    lv_t[mine] = -0.3 * total[0] / (total[1] + 1.0)

    for j in near_order:
        copy = pltpu.make_async_remote_copy(
            lv_t.at[mine], lv_t.at[mine], g_send.at[j], g_recv.at[j],
            device_id=near_peer(j), device_id_type=MESH,
        )
        copy.start()
        copies.append(copy)
    for j in range(1, 2 * n_y):
        dy, flip = j // 2, j % 2
        source = lax.rem(y + n_y - dy, n_y) * 2 + (1 - role if flip else role)
        pltpu.make_async_remote_copy(
            lv_t.at[source], lv_t.at[source], g_send.at[j], g_recv.at[j],
            device_id=near_peer(j), device_id_type=MESH,
        ).wait_recv()
    lv_out[...] = lv_t[...].reshape(width, LEAVES).T
    for copy in copies:
        copy.wait_send()


def update(x_v, onehot, lv, lv_hbm, up_hbm, up_v, sem):
    values = jnp.concatenate(split(lv[...]), axis=0)
    copies = [pltpu.make_async_copy(lv, lv_hbm, sem.at[WRITES])]
    copies[0].start()
    chunk_rows = x_v.shape[0] // WRITES
    for c in range(WRITES):
        def part(i, carry, c=c):
            at = pl.ds(pl.multiple_of(c * chunk_rows + i * 256, 256), 256)
            up_v[at, :] = x_v[at, :] + jnp.dot(onehot[at, :], values, preferred_element_type=F32)
            return carry

        lax.fori_loop(0, chunk_rows // 256, part, 0, unroll=2)
        at = pl.ds(c * chunk_rows, chunk_rows)
        copies.append(pltpu.make_async_copy(up_v.at[at], up_hbm.at[at], sem.at[c]))
        copies[-1].start()
    for copy in copies:
        copy.wait()


def solution(mesh):
    n_cls, n_rows = mesh.shape["cls"], mesh.shape["rows"]
    n_y = 4
    n_z = n_rows // n_y
    assert n_z == 16

    def per_device(logits, leaf_index, labels):
        rows, width = logits.shape
        blocks = rows // LANES
        piece = width // (2 * n_y)
        dma = pltpu.SemaphoreType.DMA
        vmem = pl.BlockSpec(memory_space=pltpu.VMEM)
        hbm = pl.BlockSpec(memory_space=pltpu.HBM)
        leaf_values, x_v, onehot = pl.pallas_call(
            functools.partial(kernel, n_cls, n_y, n_z),
            out_shape=(
                pltpu.VMEM((LEAVES, width), F32),
                pltpu.VMEM((rows, width), F32),
                pltpu.VMEM((rows, 2 * LEAVES), BF16),
            ),
            in_specs=[hbm, hbm, hbm],
            out_specs=(vmem, vmem, vmem),
            scratch_shapes=[
                pltpu.VMEM((blocks, LANES), jnp.int32),
                pltpu.VMEM((blocks, LANES), jnp.int32),
                pltpu.VMEM((width, rows), F32),
                pltpu.VMEM((2, PARTS, 2, blocks // PARTS, LANES), F32),
                pltpu.VMEM((n_cls // 2, PARTS, 2, blocks // PARTS, LANES), F32),
                pltpu.VMEM((LEAVES, rows), BF16),
                pltpu.VMEM((2, width, LEAVES), F32),
                pltpu.VMEM((2 * n_y, 2, piece, LEAVES), F32),
                pltpu.VMEM((n_z // 2, 2, piece, LEAVES), F32),
                pltpu.VMEM((2 * n_y, piece, LEAVES), F32),
                pltpu.SemaphoreType.REGULAR((3, 2)),
                dma((CHUNKS + 2,)),
                dma((PARTS,)),
                dma((PARTS,)),
                dma((n_cls // 2, PARTS)),
                dma((n_cls // 2, PARTS)),
                dma((2 * n_y,)),
                dma((2 * n_y,)),
                dma((n_z // 2,)),
                dma((n_z // 2,)),
                dma((2 * n_y,)),
                dma((2 * n_y,)),
            ],
            compiler_params=pltpu.CompilerParams(
                collective_id=0, has_side_effects=True, vmem_limit_bytes=32 * 2**20
            ),
        )(
            in_hbm(logits),
            in_hbm(leaf_index.reshape(blocks, LANES)),
            in_hbm(labels.reshape(blocks, LANES)),
        )
        return pl.pallas_call(
            update,
            out_shape=(
                pltpu.HBM((LEAVES, width), F32),
                pltpu.HBM((rows, width), F32),
            ),
            in_specs=[vmem, vmem, vmem],
            out_specs=(hbm, hbm),
            scratch_shapes=[pltpu.VMEM((rows, width), F32), dma((WRITES + 1,))],
            compiler_params=pltpu.CompilerParams(vmem_limit_bytes=16 * 2**20),
        )(x_v, onehot, leaf_values)

    return jax.shard_map(
        per_device,
        mesh=mesh,
        in_specs=(P("rows", "cls"), P("rows"), P("rows")),
        out_specs=(P(None, "cls"), P("rows", "cls")),
        check_vma=False,
    )
```

```python
import functools

import jax
import jax.numpy as jnp
from jax import lax
from jax.experimental import pallas as pl
from jax.experimental.pallas import tpu as pltpu
from jax.sharding import PartitionSpec as P

LEAVES = 128
LANES = 128
MESH = pl.DeviceIdType.MESH
F32 = jnp.float32
BF16 = jnp.bfloat16
CHUNKS = 4
PARTS = 2
TOGETHER = 4
WRITES = 8


def in_hbm(array):
    return pltpu.with_memory_space_constraint(array, pltpu.HBM)


def split(value):
    high = value.astype(BF16)
    return high, (value - high.astype(F32)).astype(BF16)


def kernel(
    n_cls, n_y, n_z,
    x_hbm, leaf_hbm, label_hbm,
    lv_out, x_v, onehot,
    leaf_v, label_v, e_v, stats, chip, onehot_t, sums, near, far, lv_t,
    known, load_sem, c_send, c_recv, s_send, s_recv, r_send, r_recv, f_send, f_recv, g_send, g_recv,
):
    row, cls = lax.axis_index("rows"), lax.axis_index("cls")
    z, y = row // n_y, row % n_y
    half, odd = z // 2, z % 2
    n_half = n_z // 2

    def role_of(of_half, of_odd):
        return jnp.where(of_half == n_half // 2, 1 - of_odd, of_odd)

    role = role_of(half, odd)
    rows, width = x_v.shape
    blocks = rows // LANES
    per_chunk = blocks // CHUNKS
    chunk_rows = rows // CHUNKS

    core = cls % 2
    n_x = n_cls // 2

    def core_peer():
        return {"rows": row, "cls": cls + 1 - 2 * core}

    def x_peer(d):
        return {"rows": row, "cls": lax.rem(cls + 2 * d, n_cls)}

    def near_place(j):
        dy, flip = j // 2, j % 2
        return lax.rem(y + dy, n_y), (1 - role if flip else role)

    def near_peer(j):
        dy, flip = j // 2, j % 2
        to_odd = 1 - odd if flip else odd
        return {"rows": (half * 2 + to_odd) * n_y + lax.rem(y + dy, n_y), "cls": cls}

    def z_peer(d):
        return {"rows": lax.rem(z + d + n_z, n_z) * n_y + y, "cls": cls}

    def far_peer(to):
        return {"rows": (to * 2 + role_of(to, role)) * n_y + y, "cls": cls}

    loads = []
    for c in range(CHUNKS):
        part = pl.ds(c * chunk_rows, chunk_rows)
        loads.append(pltpu.make_async_copy(x_hbm.at[part], x_v.at[part], load_sem.at[c]))
    loads.append(pltpu.make_async_copy(leaf_hbm, leaf_v, load_sem.at[CHUNKS]))
    loads.append(pltpu.make_async_copy(label_hbm, label_v, load_sem.at[CHUNKS + 1]))
    for load in loads:
        load.start()

    barrier = pltpu.get_barrier_semaphore()
    near_order = sorted(range(1, 2 * n_y), key=lambda j: -(min(j // 2, n_y - j // 2) + j % 2))
    for j in range(2, 2 * n_y, 2):
        pl.semaphore_signal(barrier, inc=1, device_id=near_peer(j), device_id_type=MESH)
    for d in range(1, n_x):
        pl.semaphore_signal(barrier, inc=1, device_id=x_peer(d), device_id_type=MESH)
    pl.semaphore_signal(barrier, inc=1, device_id=core_peer(), device_id_type=MESH)
    for d in (-1, 1):
        pl.semaphore_signal(barrier, inc=1, device_id=z_peer(d), device_id_type=MESH)

    def tell(step):
        for side in range(2):
            pl.semaphore_signal(
                known.at[step, side], inc=1,
                device_id=z_peer((1 - 2 * side) * 2**step), device_id_type=MESH,
            )

    def hear(step):
        for side in range(2):
            pl.semaphore_wait(known.at[step, side], 1)

    per_part = blocks // PARTS
    for c in range(CHUNKS):
        loads[c].wait()

        def local(i, carry, c=c):
            k = c * per_chunk + i
            at = pl.ds(pl.multiple_of(k * LANES, LANES), LANES)
            xt = x_v[at, :].T
            peak = jnp.max(xt, axis=0, keepdims=True)
            expo = jnp.exp(xt - peak)
            e_v[:, at] = expo
            h = c * per_chunk // per_part
            at = pl.ds(k - h * per_part, 1)
            stats[0, h, 0, at, :] = peak
            stats[0, h, 1, at, :] = jnp.sum(expo, axis=0, keepdims=True)
            return carry

        lax.fori_loop(0, per_chunk, local, 0, unroll=8)

    pl.semaphore_wait(barrier, n_x + n_y + 1)
    swaps = []
    for h in range(PARTS):
        copy = pltpu.make_async_remote_copy(
            stats.at[0, h], stats.at[1, h], c_send.at[h], c_recv.at[h],
            device_id=core_peer(), device_id_type=MESH,
        )
        copy.start()
        swaps.append(copy)
    tell(0)
    exchanges = []
    for h in range(PARTS):
        swaps[h].wait()
        peak = jnp.maximum(stats[0, h, 0], stats[1, h, 0])
        chip[0, h, 0] = peak
        chip[0, h, 1] = (
            stats[0, h, 1] * jnp.exp(stats[0, h, 0] - peak)
            + stats[1, h, 1] * jnp.exp(stats[1, h, 0] - peak)
        )
        for d in range(1, n_x):
            copy = pltpu.make_async_remote_copy(
                chip.at[0, h], chip.at[d, h], s_send.at[d, h], s_recv.at[d, h],
                device_id=x_peer(d), device_id_type=MESH,
            )
            copy.start()
            exchanges.append(copy)

    loads[CHUNKS].wait()
    loads[CHUNKS + 1].wait()

    def one_hot_t(i, carry):
        at = pl.ds(pl.multiple_of(i * LANES, LANES), LANES)
        which = lax.broadcasted_iota(jnp.int32, (LEAVES, LANES), 0)
        onehot_t[:, at] = (which == leaf_v[pl.ds(i, 1), :]).astype(F32).astype(BF16)
        return carry

    lax.fori_loop(0, blocks, one_hot_t, 0, unroll=4)

    hear(0)
    tell(1)
    piece = width // (2 * n_y)

    classes = lax.broadcasted_iota(jnp.int32, (width, LANES), 0) + cls * width
    acc = None
    for h in range(PARTS):
        for d in range(1, n_x):
            exchanges[h * (n_x - 1) + d - 1].wait()
        peak = chip[0, h, 0]
        for d in range(1, n_x):
            peak = jnp.maximum(peak, chip[d, h, 0])
        total = chip[0, h, 1] * jnp.exp(chip[0, h, 0] - peak)
        for d in range(1, n_x):
            total = total + chip[d, h, 1] * jnp.exp(chip[d, h, 0] - peak)
        stats[0, h, 1] = jnp.exp(stats[0, h, 0] - peak) / total

        for k in range(h * per_part, (h + 1) * per_part, TOGETHER):
            grads, hessians = [], []
            for i in range(k, k + TOGETHER):
                at = slice(i * LANES, (i + 1) * LANES)
                inverse = i - h * per_part
                prob = e_v[:, at] * stats[0, h, 1, inverse : inverse + 1, :]
                grads.append(prob - (classes == label_v[i : i + 1, :]).astype(F32))
                hessians.append(prob * (1.0 - prob))
            at = slice(k * LANES, (k + TOGETHER) * LANES)
            terms = split(jnp.concatenate(grads, axis=1)) + split(jnp.concatenate(hessians, axis=1))
            part = lax.dot_general(
                jnp.concatenate(terms, axis=0), onehot_t[:, at],
                (((1,), (1,)), ((), ())), preferred_element_type=F32,
            )
            acc = part if acc is None else acc + part
    sums[0] = acc[0:width] + acc[width : 2 * width]
    sums[1] = acc[2 * width : 3 * width] + acc[3 * width : 4 * width]

    shares = []
    for j in near_order:
        to_y, to_role = near_place(j)
        theirs = pl.ds(pl.multiple_of((to_y * 2 + to_role) * piece, piece), piece)
        copy = pltpu.make_async_remote_copy(
            sums.at[:, theirs], near.at[j], r_send.at[j], r_recv.at[j],
            device_id=near_peer(j), device_id_type=MESH,
        )
        copy.start()
        shares.append(copy)
    hear(1)
    tell(2)

    mine = y * 2 + role
    own_part = pl.ds(pl.multiple_of(mine * piece, piece), piece)
    for copy in shares:
        copy.wait()
    total = sums[:, own_part, :]
    for j in range(1, 2 * n_y):
        total = total + near[j]
    far[half] = total

    hear(2)
    copies = []
    for k in range(n_half - 1):
        to = jnp.where(half <= k, k + 1, k)
        copy = pltpu.make_async_remote_copy(
            far.at[half], far.at[half], f_send.at[k], f_recv.at[half],
            device_id=far_peer(to), device_id_type=MESH,
        )
        copy.start()
        copies.append(copy)

    def one_hot(i, carry):
        at = pl.ds(pl.multiple_of(i * LANES, LANES), LANES)
        hot = onehot_t[:, at].T
        onehot[at, 0:LEAVES] = hot
        onehot[at, LEAVES : 2 * LEAVES] = hot
        return carry

    lax.fori_loop(0, blocks, one_hot, 0, unroll=8)

    for d in range(1, n_half):
        source = lax.rem(half + n_half - d, n_half)
        pltpu.make_async_remote_copy(
            far.at[source], far.at[source], f_send.at[d], f_recv.at[source],
            device_id=far_peer(source), device_id_type=MESH,
        ).wait_recv()
    total = far[0]
    for k in range(1, n_half):
        total = total + far[k]
    lv_t[mine] = -0.3 * total[0] / (total[1] + 1.0)

    for j in near_order:
        copy = pltpu.make_async_remote_copy(
            lv_t.at[mine], lv_t.at[mine], g_send.at[j], g_recv.at[j],
            device_id=near_peer(j), device_id_type=MESH,
        )
        copy.start()
        copies.append(copy)
    for j in range(1, 2 * n_y):
        dy, flip = j // 2, j % 2
        source = lax.rem(y + n_y - dy, n_y) * 2 + (1 - role if flip else role)
        pltpu.make_async_remote_copy(
            lv_t.at[source], lv_t.at[source], g_send.at[j], g_recv.at[j],
            device_id=near_peer(j), device_id_type=MESH,
        ).wait_recv()
    lv_out[...] = lv_t[...].reshape(width, LEAVES).T
    for copy in copies:
        copy.wait_send()


def update(x_v, onehot, lv, lv_hbm, up_hbm, up_v, sem):
    values = jnp.concatenate(split(lv[...]), axis=0)
    copies = [pltpu.make_async_copy(lv, lv_hbm, sem.at[WRITES])]
    copies[0].start()
    chunk_rows = x_v.shape[0] // WRITES
    for c in range(WRITES):
        def part(i, carry, c=c):
            at = pl.ds(pl.multiple_of(c * chunk_rows + i * 256, 256), 256)
            up_v[at, :] = x_v[at, :] + jnp.dot(onehot[at, :], values, preferred_element_type=F32)
            return carry

        lax.fori_loop(0, chunk_rows // 256, part, 0, unroll=2)
        at = pl.ds(c * chunk_rows, chunk_rows)
        copies.append(pltpu.make_async_copy(up_v.at[at], up_hbm.at[at], sem.at[c]))
        copies[-1].start()
    for copy in copies:
        copy.wait()


def solution(mesh):
    n_cls, n_rows = mesh.shape["cls"], mesh.shape["rows"]
    n_y = 4
    n_z = n_rows // n_y
    assert n_z == 16

    def per_device(logits, leaf_index, labels):
        rows, width = logits.shape
        blocks = rows // LANES
        piece = width // (2 * n_y)
        dma = pltpu.SemaphoreType.DMA
        vmem = pl.BlockSpec(memory_space=pltpu.VMEM)
        hbm = pl.BlockSpec(memory_space=pltpu.HBM)
        leaf_values, x_v, onehot = pl.pallas_call(
            functools.partial(kernel, n_cls, n_y, n_z),
            out_shape=(
                pltpu.VMEM((LEAVES, width), F32),
                pltpu.VMEM((rows, width), F32),
                pltpu.VMEM((rows, 2 * LEAVES), BF16),
            ),
            in_specs=[hbm, hbm, hbm],
            out_specs=(vmem, vmem, vmem),
            scratch_shapes=[
                pltpu.VMEM((blocks, LANES), jnp.int32),
                pltpu.VMEM((blocks, LANES), jnp.int32),
                pltpu.VMEM((width, rows), F32),
                pltpu.VMEM((2, PARTS, 2, blocks // PARTS, LANES), F32),
                pltpu.VMEM((n_cls // 2, PARTS, 2, blocks // PARTS, LANES), F32),
                pltpu.VMEM((LEAVES, rows), BF16),
                pltpu.VMEM((2, width, LEAVES), F32),
                pltpu.VMEM((2 * n_y, 2, piece, LEAVES), F32),
                pltpu.VMEM((n_z // 2, 2, piece, LEAVES), F32),
                pltpu.VMEM((2 * n_y, piece, LEAVES), F32),
                pltpu.SemaphoreType.REGULAR((3, 2)),
                dma((CHUNKS + 2,)),
                dma((PARTS,)),
                dma((PARTS,)),
                dma((n_cls // 2, PARTS)),
                dma((n_cls // 2, PARTS)),
                dma((2 * n_y,)),
                dma((2 * n_y,)),
                dma((n_z // 2,)),
                dma((n_z // 2,)),
                dma((2 * n_y,)),
                dma((2 * n_y,)),
            ],
            compiler_params=pltpu.CompilerParams(
                collective_id=0, has_side_effects=True, vmem_limit_bytes=32 * 2**20
            ),
        )(
            in_hbm(logits),
            in_hbm(leaf_index.reshape(blocks, LANES)),
            in_hbm(labels.reshape(blocks, LANES)),
        )
        return pl.pallas_call(
            update,
            out_shape=(
                pltpu.HBM((LEAVES, width), F32),
                pltpu.HBM((rows, width), F32),
            ),
            in_specs=[vmem, vmem, vmem],
            out_specs=(hbm, hbm),
            scratch_shapes=[pltpu.VMEM((rows, width), F32), dma((WRITES + 1,))],
            compiler_params=pltpu.CompilerParams(vmem_limit_bytes=16 * 2**20),
        )(x_v, onehot, leaf_values)

    return jax.shard_map(
        per_device,
        mesh=mesh,
        in_specs=(P("rows", "cls"), P("rows"), P("rows")),
        out_specs=(P(None, "cls"), P("rows", "cls")),
        check_vma=False,
    )
```
